128 devices in a mesh: gx: 4 (over z), gy: 4 (over y), gz: 8 (over x, core).
Axes of the slice: x: 4, y: 4, z: 4, core: 2. Of those that a mesh axis runs over, the one named last changes fastest.
Arguments:
- panel: float32 [32768, 4096], P(('gx', 'gy', 'gz'))
- treat_start: int32 [32768], P(('gx', 'gy', 'gz')), may hold values from 1024 to 4096
- loading_init: float32 [64, 32768], P(None, ('gx', 'gy', 'gz'))
- factor_init: float32 [64, 4096], P(None, ('gx', 'gy', 'gz'))
- unit_init: float32 [32768], P(('gx', 'gy', 'gz'))
- day_init: float32 [4096], replicated
Outputs:
- loading_out: float32 [64, 32768], P(None, ('gx', 'gy', 'gz'))
- factor_out: float32 [64, 4096], P(None, ('gx', 'gy', 'gz'))
- unit_out: float32 [32768], P(('gx', 'gy', 'gz'))
- day_out: float32 [4096], replicated
The draws below stay inside these ranges and needn't reach their ends.
Inputs may be any that keep to these rules, and one draw needn't show every extreme that they name: A unit is treated from day treat_start on; 4096 means never treated.
All inputs are finite; a program needn't handle non-finite values.
Results may differ from the reference program's by a relative error of at most 0.0001.
Values sent between devices are 32-bit elements; how exact they have to be, the bound alone decides.
No kernel may reach another device: no remote copies, remote signals or barrier semaphores. Data moves between devices by JAX's collectives and lax.ppermute only.
A program may use at most 64 MiB of HBM per device.

```python
import jax
import jax.numpy as jnp
from jax import lax

RANK = 64
DAYS = 4096
SWEEPS = 2
UNITS = 32768


def truth_parts(key):
    keys = jax.random.split(jax.random.fold_in(key, 7), 4)
    loading_true = jax.random.normal(keys[0], (UNITS, RANK), jnp.float32)
    factor_true = jax.random.normal(keys[1], (RANK, DAYS), jnp.float32) * RANK ** (-0.5)
    unit_true = jax.random.normal(keys[2], (UNITS,), jnp.float32)
    day_true = 0.5 * jax.random.normal(keys[3], (DAYS,), jnp.float32)
    return (loading_true, factor_true, unit_true, day_true)


def draw_panel(key, part):
    loading_true, factor_true, unit_true, day_true = truth_parts(key)
    keys = jax.random.split(jax.random.fold_in(key, 11), 2)
    rising = 1.0 + 2.0 * jnp.arange(UNITS, dtype=jnp.float32) / max(UNITS - 1, 1)
    spread = jnp.exp(jax.random.uniform(keys[0], (UNITS,), jnp.float32, -1.15, 1.15))
    scales = 0.3 * rising * spread
    noise = jax.random.normal(keys[1], (UNITS, DAYS), jnp.float32)
    signal = jnp.dot(loading_true, factor_true, precision=lax.Precision.HIGHEST)
    return unit_true[:, None] + day_true[None, :] + signal + scales[:, None] * noise


def draw_loading_init(key, part):
    loading_true = truth_parts(key)[0]
    noise = jax.random.normal(jax.random.fold_in(key, 21), (UNITS, RANK), jnp.float32)
    return (loading_true + 0.5 * noise).T


def draw_factor_init(key, part):
    factor_true = truth_parts(key)[1]
    noise = jax.random.normal(jax.random.fold_in(key, 31), (RANK, DAYS), jnp.float32)
    return factor_true + 0.5 * RANK ** (-0.5) * noise


def draw_unit_init(key, part):
    unit_true = truth_parts(key)[2]
    return unit_true + 0.3 * jax.random.normal(jax.random.fold_in(key, 41), (UNITS,), jnp.float32)


def draw_day_init(key, part):
    day_true = truth_parts(key)[3]
    return day_true + 0.3 * jax.random.normal(jax.random.fold_in(key, 51), (DAYS,), jnp.float32)


def place_ends(result, rng, low, top_value):
    index_at = [jax.random.randint(jax.random.fold_in(rng, axis), (), 0, length) for axis, length in enumerate(result.shape)]
    widest = result.shape.index(max(result.shape))
    next_to = index_at[:widest] + [(index_at[widest] + 1) % result.shape[widest]] + index_at[widest + 1:]
    return result.at[tuple(index_at)].set(low).at[tuple(next_to)].set(top_value)


def setup_inputs(seed: int = 0) -> dict:
    streams_of = jax.random.split(jax.random.key(seed), 7)
    panel = draw_panel(jax.random.fold_in(streams_of[6], 71), 0)
    treat_start = place_ends(jax.random.randint(streams_of[1], (UNITS,), DAYS // 4, DAYS + 1), jax.random.fold_in(streams_of[1], 1), DAYS // 4, DAYS).astype(jnp.int32)
    loading_init = draw_loading_init(jax.random.fold_in(streams_of[6], 71), 0)
    factor_init = draw_factor_init(jax.random.fold_in(streams_of[6], 71), 0)
    unit_init = draw_unit_init(jax.random.fold_in(streams_of[6], 71), 0)
    day_init = draw_day_init(jax.random.fold_in(streams_of[6], 71), 0)
    return {"panel": panel, "treat_start": treat_start, "loading_init": loading_init, "factor_init": factor_init, "unit_init": unit_init, "day_init": day_init}


RIDGE = 1.0

def solve_spd(matrix, right):
    lower = jnp.linalg.cholesky(matrix)
    middle = lax.linalg.triangular_solve(lower, right, left_side=True, lower=True)
    return lax.linalg.triangular_solve(lower, middle, left_side=True, lower=True, transpose_a=True)

def reference(panel, treat_start, loading_init, factor_init, unit_init, day_init):
    loading = loading_init
    factors = factor_init
    unit_eff = unit_init
    day_eff = day_init
    ridge_eye = jnp.eye(RANK, dtype=jnp.float32) * RIDGE
    observed = lax.broadcasted_iota(jnp.int32, (UNITS, DAYS), 1) < treat_start[:, None]
    for sweep_index in range(SWEEPS):
        fitted = lax.dot_general(loading.astype(jnp.float32), factors.astype(jnp.float32), (((0,), (0,)), ((), ())), precision=lax.Precision.HIGHEST, preferred_element_type=jnp.float32)
        imputed = jnp.where(observed, panel, unit_eff[:, None] + day_eff[None, :] + fitted)
        without = imputed - fitted
        day_sums = jnp.sum(without, 0)
        row_sums = jnp.sum(without, 1)
        grand = jnp.sum(day_sums) / (UNITS * DAYS)
        day_eff = day_sums / UNITS - grand
        unit_eff = row_sums / DAYS - grand
        resid = imputed - unit_eff[:, None] - day_eff[None, :]
        unit_gram = jnp.dot(loading, loading.T, precision=lax.Precision.HIGHEST)
        weighted = jnp.dot(loading, resid, precision=lax.Precision.HIGHEST)
        factors = solve_spd(unit_gram + ridge_eye, weighted)
        factor_gram = jnp.dot(factors, factors.T, precision=lax.Precision.HIGHEST)
        projected = lax.dot_general(factors.astype(jnp.float32), resid.astype(jnp.float32), (((1,), (1,)), ((), ())), precision=lax.Precision.HIGHEST, preferred_element_type=jnp.float32)
        loading = solve_spd(factor_gram + ridge_eye, projected)
    return (loading, factors, unit_eff, day_eff)
```

```python
import functools

import jax
import jax.numpy as jnp
from jax import lax
from jax.experimental import pallas as pl
from jax.experimental.pallas import tpu as pltpu
from jax.sharding import Mesh
from jax.sharding import PartitionSpec as P

SWEEPS = 2
RIDGE = 1.0
GX_GY_GZ = ("gx", "gy", "gz_0", "gz_1")
CHIPS = ("gx", "gy", "gz_0")
CORE = "gz_1"

RANK = 64
ROWS = 256
DAYS = 4096
HALF = 2048
UNITS = 32768
BLK = 512
NBLK = HALF // BLK
PEERS = 64
CHUNK = 17
BROWS = 16 * CHUNK
PAY = PEERS * CHUNK
F32 = jnp.float32
BF = jnp.bfloat16


def dot(x, y, dims=((1,), (0,))):
    return lax.dot_general(x, y, (dims, ((), ())), preferred_element_type=F32)


def dot_exact(x, y, dims=((1,), (0,))):
    return lax.dot_general(x, y, (dims, ((), ())), preferred_element_type=F32, precision=lax.Precision.HIGHEST)


def split(x):
    hi = x.astype(BF)
    return hi, (x - hi.astype(F32)).astype(BF)


def split_rows(x):
    hi = x.astype(BF).astype(F32)
    mid = (x - hi).astype(BF).astype(F32)
    return [hi, mid, x - hi - mid]


def inverse(m):
    n = m.shape[0]
    row = lax.broadcasted_iota(jnp.int32, (n, n), 0)
    col = lax.broadcasted_iota(jnp.int32, (n, n), 1)
    w = jnp.concatenate([m, (row == col).astype(F32)], axis=1)
    rows = lax.broadcasted_iota(jnp.int32, (n, 1), 0)
    for k in range(n):
        c = w[:, k : k + 1]
        r = w[k : k + 1, :] / w[k : k + 1, k : k + 1]
        w = jnp.where(rows == k, r, w - c * r)
    return w[:, n:]


def first_kernel(k_ref, panel, f, b, l, a, ts, acc_in, out, dhi, dlo, acc, lt, lw, gp, tsb, *, own):
    j = pl.program_id(0)

    @pl.when(j == 0)
    def _():
        lv = l[...]
        lhi, llo = split(lv)
        hi32, lo32 = lhi.astype(F32), llo.astype(F32)
        ones = jnp.ones((3, ROWS), F32)
        k_rows = [hi32, hi32, lo32] + split_rows(a[...]) + [ones, jnp.zeros((58, ROWS), F32)]
        lt[...] = jnp.concatenate(k_rows, axis=0).T.astype(BF)
        lw[0:64] = lhi
        lw[64:128] = llo
        lw[128:144] = jnp.ones((16, ROWS), BF)
        g = dot_exact(lv, lv, ((1,), (1,)))
        gp[...] = jnp.concatenate([g[0:32], g[32:64]], axis=1)
        tsb[...] = jnp.broadcast_to(ts[...].astype(F32), (128, ROWS)).T
        acc[...] = acc_in[...]

    k = k_ref[0]
    half = k if own else 1 - k
    fhi, flo = split(f[...])
    aux = jnp.concatenate([jnp.ones((3, BLK), F32)] + split_rows(b[...]) + [jnp.zeros((58, BLK), F32)], axis=0)
    fa = jnp.concatenate([fhi, flo, fhi, aux.astype(BF)], axis=0)
    s = dot(lt[...], fa)
    day = (lax.broadcasted_iota(jnp.int32, (ROWS, 128), 1) + (half * HALF + j * BLK)).astype(F32)
    left = tsb[...] - day
    run = acc[...]
    for q in range(BLK // 128):
        cols = slice(128 * q, 128 * (q + 1))
        d = jnp.where(left > 128.0 * q, panel[:, cols] - s[:, cols], 0.0)
        hi, lo = split(d)
        dhi[:, cols] = hi
        dlo[:, cols] = lo
        run = run + d
    acc[...] = run
    r1 = dot(lw[...], dhi[...])
    w = r1[0:64] + r1[64:128]
    r2 = dot(lw[...], dlo[...])
    w = w + r2[0:64]
    day_sum = r1[128:129] + r2[128:129]
    means = dot_exact(jnp.ones((8, 128), F32), run, ((1,), (1,))) * (1.0 / DAYS)
    if not own:
        means = means * 0.0
    lv = l[...]
    l1 = dot_exact(jnp.ones((8, ROWS), F32), lv, ((1,), (1,)))[0:1]
    lr = dot_exact(means, lv, ((1,), (1,)))[0:1]
    a_sum = jnp.broadcast_to(jnp.sum(a[...], axis=1, keepdims=True), (1, 128))
    extra = [day_sum[:, 128 * q : 128 * (q + 1)] for q in range(4)]
    extra += [gp[pl.ds(pl.multiple_of(8 * j, 8), 8), :], jnp.concatenate([l1, lr], axis=1), a_sum]
    extra = jnp.concatenate(extra + [jnp.zeros((2, 128), F32)], axis=0)
    for i in range(8):
        for t in range(2):
            at = CHUNK * (2 * i + t)
            out[at : at + 8, :] = w[8 * i : 8 * i + 8, 256 * t : 256 * t + 128]
            out[at + 8 : at + 16, :] = w[8 * i : 8 * i + 8, 256 * t + 128 : 256 * t + 256]
            out[at + 16 : at + 17, :] = extra[2 * i + t : 2 * i + t + 1]


def first_half(k, panel, f, b, l, a, ts, acc, own):
    def panel_at(j, k_ref):
        half = k_ref[0] if own else 1 - k_ref[0]
        return (0, half * NBLK + j)

    whole = lambda shape: pl.BlockSpec(shape, lambda j, k_ref: (0, 0))
    along = lambda rows: pl.BlockSpec((rows, BLK), lambda j, k_ref: (0, j))
    return pl.pallas_call(
        functools.partial(first_kernel, own=own),
        grid_spec=pltpu.PrefetchScalarGridSpec(
            num_scalar_prefetch=1,
            grid=(NBLK,),
            in_specs=[
                pl.BlockSpec((ROWS, BLK), panel_at),
                along(RANK),
                along(1),
                whole((RANK, ROWS)),
                whole((1, ROWS)),
                whole((1, ROWS)),
                whole((ROWS, 128)),
            ],
            out_specs=[
                pl.BlockSpec((BROWS, 128), lambda j, k_ref: (j, 0)),
                along(ROWS),
                along(ROWS),
                whole((ROWS, 128)),
            ],
            scratch_shapes=[
                pltpu.VMEM((ROWS, 256), BF),
                pltpu.VMEM((144, ROWS), BF),
                pltpu.VMEM((32, 128), F32),
                pltpu.VMEM((ROWS, 128), F32),
            ],
        ),
        out_shape=[
            jax.ShapeDtypeStruct((PAY, 128), F32),
            jax.ShapeDtypeStruct((ROWS, HALF), BF),
            jax.ShapeDtypeStruct((ROWS, HALF), BF),
            jax.ShapeDtypeStruct((ROWS, 128), F32),
        ],
        name="first_own" if own else "first_other",
    )(k, panel, f, b, l, a, ts, acc)


def vmem():
    return pl.BlockSpec(memory_space=pltpu.VMEM)


def sum_kernel(x, out):
    total = x[0:CHUNK, :]
    for c in range(1, PEERS):
        total = total + x[CHUNK * c : CHUNK * (c + 1), :]
    for c in range(PEERS):
        out[CHUNK * c : CHUNK * (c + 1), :] = total


def sum_and_copy(x):
    return pl.pallas_call(
        sum_kernel,
        in_specs=[vmem()],
        out_specs=vmem(),
        out_shape=jax.ShapeDtypeStruct((PAY, 128), F32),
        name="sum_and_copy",
    )(x)


def extra_row(x, j, e):
    at = BROWS * j + CHUNK * e + 16
    return x[at : at + 1, :]


def gram_kernel(x, out):
    packed = jnp.concatenate([extra_row(x, j, 4 + e) for j in range(4) for e in range(8)], axis=0)
    g = jnp.concatenate([packed[:, 0:64], packed[:, 64:128]], axis=0)
    row = lax.broadcasted_iota(jnp.int32, (RANK, RANK), 0)
    col = lax.broadcasted_iota(jnp.int32, (RANK, RANK), 1)
    out[...] = inverse(g + jnp.where(row == col, RIDGE, 0.0))


def gram_inverse(x):
    return pl.pallas_call(
        gram_kernel,
        in_specs=[vmem()],
        out_specs=vmem(),
        out_shape=jax.ShapeDtypeStruct((RANK, RANK), F32),
        name="gram_inverse",
    )(x)


def second_kernel(own, oth, ginv, f_own, f_oth, b_own, b_oth, dhi_own, dlo_own, dhi_oth, dlo_oth, l, a, acc,
                  fn_own, fn_oth, bn_own, bn_oth, ln, an):
    sums = [jnp.concatenate([extra_row(x, j, q) for j in range(4) for q in range(4)], axis=1) for x in (own, oth)]
    mean_d = (jnp.sum(sums[0], axis=1, keepdims=True) + jnp.sum(sums[1], axis=1, keepdims=True)) * (1.0 / (UNITS * DAYS))
    mean_b = (jnp.sum(b_own[...], axis=1, keepdims=True) + jnp.sum(b_oth[...], axis=1, keepdims=True)) * (1.0 / DAYS)
    mean_a = extra_row(own, 3, 13)[:, 0:1] * (1.0 / UNITS)
    lane = lax.broadcasted_iota(jnp.int32, (1, 128), 1)
    l_own, l_oth = extra_row(own, 3, 12), extra_row(oth, 3, 12)
    lines = l_own + jnp.where(lane >= 64, l_oth, 0.0)
    turned = jnp.broadcast_to(lines, (128, 128)).T
    l1 = turned[0:64, 0:1]
    u = (mean_d + mean_a) * l1 - turned[64:128, 0:1]
    ghi, glo = split(ginv[...])
    gcat = jnp.concatenate([ghi, ghi, glo], axis=1)
    h = jnp.zeros((RANK, 2 * RANK), F32)
    zt = jnp.zeros((ROWS, RANK), F32)
    f1 = jnp.zeros((RANK, 1), F32)
    fb = jnp.zeros((RANK, 1), F32)
    for x, f, b, dhi, dlo, fn, bn, col in (
        (own, f_own, b_own, dhi_own, dlo_own, fn_own, bn_own, sums[0]),
        (oth, f_oth, b_oth, dhi_oth, dlo_oth, fn_oth, bn_oth, sums[1]),
    ):
        v = mean_d + mean_b - col * (1.0 / UNITS)
        bn[...] = b[...] - v
        for j in range(NBLK):
            cols = slice(BLK * j, BLK * (j + 1))
            lines = []
            for i in range(8):
                tiles = []
                for t in range(2):
                    at = BROWS * j + CHUNK * (2 * i + t)
                    tiles += [x[at : at + 8, :], x[at + 8 : at + 16, :]]
                lines.append(jnp.concatenate(tiles, axis=1))
            w = jnp.concatenate(lines, axis=0)
            fv = f[:, cols]
            vb = v[:, cols]
            r = w + u + l1 * vb - fv
            rhi, rlo = split(r)
            new = fv + dot(gcat, jnp.concatenate([rhi, rlo, rhi], axis=0))
            fn[:, cols] = new
            nhi, nlo = split(new)
            ohi, olo = split(fv)
            his = jnp.concatenate([nhi, ohi], axis=0)
            los = jnp.concatenate([nlo, olo], axis=0)
            last = ((1,), (1,))
            h = h + dot(nhi, his, last) + dot(nhi, los, last) + dot(nlo, his, last)
            both = jnp.concatenate([nhi, nlo], axis=0)
            z = dot(dhi[:, cols], both, last)
            zt = zt + z[:, 0:64] + z[:, 64:128] + dot(dlo[:, cols], nhi, last)
            f1 = f1 + jnp.sum(new, axis=1, keepdims=True)
            fb = fb + jnp.sum(new * vb, axis=1, keepdims=True)
    means = dot_exact(jnp.ones((8, 128), F32), acc[...], ((1,), (1,)))[0:1] * (1.0 / DAYS)
    da = mean_d + mean_a - means
    an[...] = a[...] - da
    row = lax.broadcasted_iota(jnp.int32, (RANK, RANK), 0)
    col = lax.broadcasted_iota(jnp.int32, (RANK, RANK), 1)
    hinv = inverse(h[:, 0:64] + jnp.where(row == col, RIDGE, 0.0))
    p = dot_exact(h[:, 64:128], l[...]) + f1 * da + fb + zt.T
    ln[...] = dot_exact(hinv, p)


def second(*operands):
    return pl.pallas_call(
        second_kernel,
        in_specs=[vmem()] * len(operands),
        out_specs=[vmem()] * 6,
        out_shape=[
            jax.ShapeDtypeStruct((RANK, HALF), F32),
            jax.ShapeDtypeStruct((RANK, HALF), F32),
            jax.ShapeDtypeStruct((1, HALF), F32),
            jax.ShapeDtypeStruct((1, HALF), F32),
            jax.ShapeDtypeStruct((RANK, ROWS), F32),
            jax.ShapeDtypeStruct((1, ROWS), F32),
        ],
        name="second",
    )(*operands)


def pack_kernel(x, out):
    v = x[...]
    packed = jnp.concatenate([v[16 * q : 16 * q + 16] for q in range(4)], axis=1)
    for c in range(PEERS):
        out[16 * c : 16 * c + 16, :] = packed


def unpack_kernel(k_ref, own, oth, f_own, f_oth):
    k = k_ref[0]
    even = k == 0
    lane = lax.broadcasted_iota(jnp.int32, (16, 128), 1)
    for j in range(16):
        for dst, half in ((f_own, k), (f_oth, 1 - k)):
            parts = []
            for m in range(4):
                at = pl.multiple_of((half * 32 + 2 * j + m // 2) * 16, 16)
                x, y = own[pl.ds(at, 16), :], oth[pl.ds(at, 16), :]
                parts.append(jnp.where(even, x, y) if m % 2 == 0 else jnp.where(even, y, x))
            for q in range(4):
                total = jnp.zeros((16, 128), F32)
                for m in range(4):
                    moved = pltpu.roll(parts[m], (32 * (m - q)) % 128, 1) if m != q else parts[m]
                    total = jnp.where((lane >= 32 * m) & (lane < 32 * m + 32), moved, total)
                dst[16 * q : 16 * q + 16, 128 * j : 128 * j + 128] = total


def gather_factors(k, f):
    lines = pl.pallas_call(
        pack_kernel,
        in_specs=[vmem()],
        out_specs=vmem(),
        out_shape=jax.ShapeDtypeStruct((PEERS * 16, 128), F32),
        name="pack_factors",
    )(f)
    own = swap_chips(lines)
    oth = other_core(own)
    return pl.pallas_call(
        unpack_kernel,
        in_specs=[pl.BlockSpec(memory_space=pltpu.SMEM), vmem(), vmem()],
        out_specs=[vmem(), vmem()],
        out_shape=[jax.ShapeDtypeStruct((RANK, HALF), F32)] * 2,
        name="unpack_factors",
    )(k, own, oth)


def swap_chips(lines):
    shape = lines.shape
    parts = lines.reshape(PEERS, 1, -1)
    return lax.all_to_all(parts, CHIPS, 0, 0, tiled=True).reshape(shape)


def other_core(x):
    return lax.ppermute(x, CORE, [(0, 1), (1, 0)])


def body(panel, treat_start, loading_init, factor_init, unit_init, day_init):
    core = lax.axis_index(CORE)
    k = core.astype(jnp.int32).reshape(1)
    f_own, f_oth = gather_factors(k, factor_init)
    loading = loading_init
    a = unit_init.reshape(1, ROWS)
    ts = treat_start.reshape(1, ROWS)
    b = day_init.reshape(2, HALF)
    b_own = lax.dynamic_slice_in_dim(b, core, 1, 0)
    b_oth = lax.dynamic_slice_in_dim(b, 1 - core, 1, 0)
    zero = jnp.zeros((ROWS, 128), F32)
    for _ in range(SWEEPS):
        sent, dhi_oth, dlo_oth, acc = first_half(k, panel, f_oth, b_oth, loading, a, ts, zero, False)
        arrived = other_core(sent)
        kept, dhi_own, dlo_own, acc = first_half(k, panel, f_own, b_own, loading, a, ts, acc, True)
        summed = sum_and_copy(swap_chips(kept + arrived))
        own = swap_chips(summed)
        oth = other_core(own)
        ginv = gram_inverse(own)
        f_own, f_oth, b_own, b_oth, loading, a = second(
            own, oth, ginv, f_own, f_oth, b_own, b_oth, dhi_own, dlo_own, dhi_oth, dlo_oth, loading, a, acc
        )
    chip = lax.axis_index(CHIPS)
    device = 2 * chip + core
    in_own = (device // 64) == core
    source = jnp.where(in_own, f_own, f_oth)
    factors = lax.dynamic_slice_in_dim(source, (device % 64) * 32, 32, 1)
    b_all = jnp.where(core == 0, jnp.concatenate([b_own, b_oth], 1), jnp.concatenate([b_oth, b_own], 1))
    return (loading, factors, a.reshape(ROWS), b_all.reshape(DAYS))


def solution(mesh):
    finer = Mesh(
        mesh.devices.reshape(mesh.shape["gx"], mesh.shape["gy"], 4, 2), ("gx", "gy", "gz_0", "gz_1")
    )
    return jax.shard_map(
        body,
        mesh=finer,
        in_specs=(
            P(GX_GY_GZ, None),
            P(GX_GY_GZ),
            P(None, GX_GY_GZ),
            P(None, GX_GY_GZ),
            P(GX_GY_GZ),
            P(),
        ),
        out_specs=(P(None, GX_GY_GZ), P(None, GX_GY_GZ), P(GX_GY_GZ), P()),
        check_vma=False,
    )
```

```python
import functools

import jax
import jax.numpy as jnp
from jax import lax
from jax.experimental import pallas as pl
from jax.experimental.pallas import tpu as pltpu
from jax.sharding import Mesh
from jax.sharding import PartitionSpec as P

SWEEPS = 2
RIDGE = 1.0
GX_GY_GZ = ("gx", "gy", "gz_0", "gz_1")
CHIPS = ("gx", "gy", "gz_0")
CORE = "gz_1"

RANK = 64
ROWS = 256
DAYS = 4096
HALF = 2048
UNITS = 32768
BLK = 512
NBLK = HALF // BLK
PEERS = 64
CHUNK = 17
BROWS = 16 * CHUNK
PAY = PEERS * CHUNK
F32 = jnp.float32
BF = jnp.bfloat16


def dot(x, y, dims=((1,), (0,))):
    return lax.dot_general(x, y, (dims, ((), ())), preferred_element_type=F32)


def dot_exact(x, y, dims=((1,), (0,))):
    return lax.dot_general(x, y, (dims, ((), ())), preferred_element_type=F32, precision=lax.Precision.HIGHEST)


def split(x):
    hi = x.astype(BF)
    return hi, (x - hi.astype(F32)).astype(BF)


def split_rows(x):
    hi = x.astype(BF).astype(F32)
    mid = (x - hi).astype(BF).astype(F32)
    return [hi, mid, x - hi - mid]


def square_inverse(p):
    (a, b), (c, d) = p
    q = 1.0 / (a * d - b * c)
    return [[d * q, -b * q], [-c * q, a * q]]


def mul(x, y):
    return [[x[i][0] * y[0][j] + x[i][1] * y[1][j] for j in range(2)] for i in range(2)]


def block_inverse(p):
    a, b, c, d = [[[p[i + r][j + t] for t in range(2)] for r in range(2)] for i in (0, 2) for j in (0, 2)]
    ai = square_inverse(a)
    ca = mul(c, ai)
    cab = mul(ca, b)
    s = square_inverse([[d[i][j] - cab[i][j] for j in range(2)] for i in range(2)])
    ab = mul(ai, b)
    abs_ = mul(ab, s)
    corner = mul(abs_, ca)
    sca = mul(s, ca)
    top = [[ai[i][0] + corner[i][0], ai[i][1] + corner[i][1], -abs_[i][0], -abs_[i][1]] for i in range(2)]
    return top + [[-sca[i][0], -sca[i][1], s[i][0], s[i][1]] for i in range(2)]


def inverse(m):
    n = m.shape[0]
    row = lax.broadcasted_iota(jnp.int32, (n, n), 0)
    col = lax.broadcasted_iota(jnp.int32, (n, n), 1)
    w = jnp.concatenate([m, (row == col).astype(F32)], axis=1)
    w = [w[8 * t : 8 * t + 8] for t in range(n // 8)]
    rows = lax.broadcasted_iota(jnp.int32, (8, 2 * n), 0)
    for k in range(0, n, 4):
        at, r0 = k // 8, k % 8
        c = [[jnp.broadcast_to(v[:, k + j : k + j + 1], (8, 2 * n)) for j in range(4)] for v in w]
        lines = [w[at][r0 + i : r0 + i + 1] for i in range(4)]
        p = block_inverse([[c[at][j][r0 + i : r0 + i + 1] for j in range(4)] for i in range(4)])
        t = [p[i][0] * lines[0] + p[i][1] * lines[1] + (p[i][2] * lines[2] + p[i][3] * lines[3]) for i in range(4)]
        for g in range(n // 8):
            w[g] = w[g] - ((c[g][0] * t[0] + c[g][1] * t[1]) + (c[g][2] * t[2] + c[g][3] * t[3]))
        for i in range(4):
            w[at] = jnp.where(rows == r0 + i, t[i], w[at])
    return jnp.concatenate(w, axis=0)[:, n:]


def first_kernel(k_ref, panel, f, b, l, a, *rest, own):
    if own:
        ts, acc_in, lt, lw, gp, tsb, out, dhi, dlo, rm = rest
    else:
        ts, out, dhi, dlo, acc_out, lt, lw, gp, tsb = rest
        lv = l[...]
        lhi, llo = split(lv)
        hi32, lo32 = lhi.astype(F32), llo.astype(F32)
        ones = jnp.ones((3, ROWS), F32)
        k_rows = [hi32, hi32, lo32] + split_rows(a[...]) + [ones, jnp.zeros((58, ROWS), F32)]
        lt[...] = jnp.concatenate(k_rows, axis=0).T.astype(BF)
        lw[0:64] = lhi
        lw[64:128] = llo
        lw[128:144] = jnp.ones((16, ROWS), BF)
        last = ((1,), (1,))
        both = jnp.concatenate([lhi, llo], axis=0)
        g = dot(both, lhi, last)
        g = g[0:64] + g[64:128] + dot(lhi, llo, last)
        gp[0:32] = jnp.concatenate([g[0:32], g[32:64]], axis=1)
        l1 = dot(jnp.ones((16, ROWS), BF), both, last)[0:1]
        gp[32:33] = jnp.concatenate([l1[:, 0:64] + l1[:, 64:128], jnp.zeros((1, 64), F32)], axis=1)
        tsb[...] = jnp.broadcast_to(ts[...].astype(F32), (128, ROWS)).T

    k = k_ref[0]
    half = k if own else 1 - k
    start = pl.multiple_of(half * HALF, HALF)
    lane = lax.broadcasted_iota(jnp.int32, (ROWS, 128), 1)
    left = tsb[...] - (lane + start).astype(F32)
    run = acc_in[...] if own else jnp.zeros((ROWS, 128), F32)
    a_sum = jnp.broadcast_to(jnp.sum(a[...], axis=1, keepdims=True), (1, 128))
    for j in range(NBLK):
        whole = slice(BLK * j, BLK * (j + 1))
        fhi, flo = split(f[:, whole])
        bv = b[:, pl.ds(start + BLK * j, BLK)]
        aux = jnp.concatenate([jnp.ones((3, BLK), F32)] + split_rows(bv) + [jnp.zeros((58, BLK), F32)], axis=0)
        fa = jnp.concatenate([fhi, flo, fhi, aux.astype(BF)], axis=0)
        s = dot(lt[...], fa)
        for q in range(BLK // 128):
            at = BLK * j + 128 * q
            cols = slice(at, at + 128)
            x = panel[:, pl.ds(start + at, 128)]
            d = jnp.where(left > float(at), x - s[:, 128 * q : 128 * (q + 1)], 0.0)
            hi, lo = split(d)
            dhi[:, cols] = hi
            dlo[:, cols] = lo
            run = run + d
        r1 = dot(lw[...], dhi[:, whole])
        r2 = dot(lw[...], dlo[:, whole])
        w = r1[0:64] + r1[64:128] + r2[0:64]
        day_sum = r1[128:129] + r2[128:129]
        extra = [day_sum[:, 128 * q : 128 * (q + 1)] for q in range(4)]
        line = gp[32:33, :]
        if own and j == NBLK - 1:
            means = dot_exact(jnp.ones((8, 128), F32), run, ((1,), (1,))) * (1.0 / DAYS)
            rm[...] = means[0:1]
            lr = dot_exact(means, l[...], ((1,), (1,)))[0:1]
            line = jnp.concatenate([line[:, 0:64], lr], axis=1)
        extra += [gp[8 * j : 8 * j + 8], line, a_sum, jnp.zeros((2, 128), F32)]
        extra = jnp.concatenate(extra, axis=0)
        for i in range(8):
            for t in range(2):
                at = BROWS * j + CHUNK * (2 * i + t)
                out[at : at + 8, :] = w[8 * i : 8 * i + 8, 256 * t : 256 * t + 128]
                out[at + 8 : at + 16, :] = w[8 * i : 8 * i + 8, 256 * t + 128 : 256 * t + 256]
                out[at + 16 : at + 17, :] = extra[2 * i + t : 2 * i + t + 1]
    if not own:
        acc_out[...] = run


def vmem():
    return pl.BlockSpec(memory_space=pltpu.VMEM)


def smem():
    return pl.BlockSpec(memory_space=pltpu.SMEM)


def call(kernel, name, scalars, operands, outs, scratch=()):
    return pl.pallas_call(
        kernel,
        in_specs=[smem()] * len(scalars) + [vmem()] * len(operands),
        out_specs=[vmem()] * len(outs),
        out_shape=[pltpu.VMEM(shape, dtype) for shape, dtype in outs],
        scratch_shapes=list(scratch),
        compiler_params=pltpu.CompilerParams(vmem_limit_bytes=16 << 20),
        name=name,
    )(*scalars, *[pltpu.with_memory_space_constraint(x, pltpu.VMEM) for x in operands])


def first_other(k, panel, f, b, l, a, ts):
    outs = [((PAY, 128), F32), ((ROWS, HALF), BF), ((ROWS, HALF), BF), ((ROWS, 128), F32)]
    outs += [((ROWS, 256), BF), ((144, ROWS), BF), ((40, 128), F32), ((ROWS, 128), F32)]
    return call(functools.partial(first_kernel, own=False), "first_other", [k], [panel, f, b, l, a, ts], outs)


def first_own(k, panel, f, b, l, a, ts, *rest):
    outs = [((PAY, 128), F32), ((ROWS, HALF), BF), ((ROWS, HALF), BF), ((1, ROWS), F32)]
    return call(functools.partial(first_kernel, own=True), "first_own", [k], [panel, f, b, l, a, ts, *rest], outs)


def sum_kernel(x, out):
    slab = x[0 : 8 * CHUNK, :]
    for g in range(1, 8):
        slab = slab + x[8 * CHUNK * g : 8 * CHUNK * (g + 1), :]
    total = slab[0:CHUNK]
    for c in range(1, 8):
        total = total + slab[CHUNK * c : CHUNK * (c + 1)]
    slab = jnp.concatenate([total] * 8, axis=0)
    for g in range(8):
        out[8 * CHUNK * g : 8 * CHUNK * (g + 1), :] = slab


def sum_and_copy(x):
    return call(sum_kernel, "sum_and_copy", [], [x], [((PAY, 128), F32)])[0]


def extra_row(x, j, e):
    at = BROWS * j + CHUNK * e + 16
    return x[at : at + 1, :]


def gram_kernel(x, out):
    packed = jnp.concatenate([extra_row(x, j, 4 + e) for j in range(4) for e in range(8)], axis=0)
    g = jnp.concatenate([packed[:, 0:64], packed[:, 64:128]], axis=0)
    row = lax.broadcasted_iota(jnp.int32, (RANK, RANK), 0)
    col = lax.broadcasted_iota(jnp.int32, (RANK, RANK), 1)
    out[...] = inverse(g + jnp.where(row == col, RIDGE, 0.0))


def gram_inverse(x):
    return call(gram_kernel, "gram_inverse", [], [x], [((RANK, RANK), F32)])[0]


def second_kernel(k_ref, own, oth, ginv, f_own, f_oth, b_ref, dhi_own, dlo_own, dhi_oth, dlo_oth, l, a, rm,
                  fn_own, fn_oth, bn, ln, an, shard, turn):
    k = k_ref[0]
    starts = [pl.multiple_of(k * HALF, HALF), pl.multiple_of((1 - k) * HALF, HALF)]
    sums = [jnp.concatenate([extra_row(x, j, q) for j in range(4) for q in range(4)], axis=1) for x in (own, oth)]
    mean_d = jnp.sum(sums[0] + sums[1], axis=1, keepdims=True) * (1.0 / (UNITS * DAYS))
    mean_b = jnp.sum(b_ref[...], axis=1, keepdims=True) * (1.0 / DAYS)
    mean_a = extra_row(own, 3, 13)[:, 0:1] * (1.0 / UNITS)
    lane = lax.broadcasted_iota(jnp.int32, (1, 128), 1)
    l_own, l_oth = extra_row(own, 3, 12), extra_row(oth, 3, 12)
    lines = l_own + jnp.where(lane >= 64, l_oth, 0.0)
    turned = jnp.broadcast_to(lines, (128, 128)).T
    l1 = turned[0:64, 0:1]
    u = (mean_d + mean_a) * l1 - turned[64:128, 0:1]
    ghi, glo = split(ginv[...])
    gcat = jnp.concatenate([ghi, ghi, glo], axis=1)
    h = jnp.zeros((RANK, 2 * RANK), F32)
    zt = jnp.zeros((ROWS, RANK), F32)
    f1 = jnp.zeros((RANK, 128), F32)
    fb = jnp.zeros((RANK, 128), F32)
    last = ((1,), (1,))
    for x, f, dhi, dlo, fn, col, start in (
        (own, f_own, dhi_own, dlo_own, fn_own, sums[0], starts[0]),
        (oth, f_oth, dhi_oth, dlo_oth, fn_oth, sums[1], starts[1]),
    ):
        v = mean_d + mean_b - col * (1.0 / UNITS)
        bn[:, pl.ds(start, HALF)] = b_ref[:, pl.ds(start, HALF)] - v
        for j in range(NBLK):
            cols = slice(BLK * j, BLK * (j + 1))
            lines = []
            for i in range(8):
                tiles = []
                for t in range(2):
                    at = BROWS * j + CHUNK * (2 * i + t)
                    tiles += [x[at : at + 8, :], x[at + 8 : at + 16, :]]
                lines.append(jnp.concatenate(tiles, axis=1))
            w = jnp.concatenate(lines, axis=0)
            fv = f[:, cols]
            vb = v[:, cols]
            r = w + u + l1 * vb - fv
            rhi, rlo = split(r)
            new = fv + dot(gcat, jnp.concatenate([rhi, rlo, rhi], axis=0))
            fn[:, cols] = new
            nhi, nlo = split(new)
            ohi, olo = split(fv)
            his = jnp.concatenate([nhi, ohi], axis=0)
            los = jnp.concatenate([nlo, olo], axis=0)
            h = h + dot(nhi, his, last) + dot(nhi, los, last) + dot(nlo, his, last)
            both = jnp.concatenate([nhi, nlo], axis=0)
            z = dot(dhi[:, cols], both, last)
            zt = zt + z[:, 0:64] + z[:, 64:128] + dot(dlo[:, cols], nhi, last)
            nb = new * vb
            for q in range(BLK // 128):
                f1 = f1 + new[:, 128 * q : 128 * (q + 1)]
                fb = fb + nb[:, 128 * q : 128 * (q + 1)]
    f1 = jnp.sum(f1, axis=1, keepdims=True)
    fb = jnp.sum(fb, axis=1, keepdims=True)
    da = mean_d + mean_a - rm[...]
    an[...] = a[...] - da
    row = lax.broadcasted_iota(jnp.int32, (RANK, RANK), 0)
    col = lax.broadcasted_iota(jnp.int32, (RANK, RANK), 1)
    hinv = inverse(h[:, 0:64] + jnp.where(row == col, RIDGE, 0.0))
    p = dot_exact(h[:, 64:128], l[...]) + f1 * da + fb + zt.T
    ln[...] = dot_exact(hinv, p)
    tile = pl.multiple_of(128 * k_ref[2], 128)
    mine = jnp.where(k_ref[1] == 1, fn_own[:, pl.ds(tile, 128)], fn_oth[:, pl.ds(tile, 128)])
    turn[...] = mine.T
    shard[...] = turn[pl.ds(pl.multiple_of(32 * k_ref[3], 32), 32), :]


def second(k, *operands):
    outs = [((RANK, HALF), F32), ((RANK, HALF), F32), ((1, DAYS), F32), ((RANK, ROWS), F32), ((1, ROWS), F32)]
    return call(second_kernel, "second", [k], operands, outs + [((32, RANK), F32)], [pltpu.VMEM((128, RANK), F32)])


def pack_kernel(x, out):
    v = x[...].T
    packed = jnp.concatenate([v[16 * q : 16 * q + 16] for q in range(4)], axis=1)
    for c in range(PEERS):
        out[16 * c : 16 * c + 16, :] = packed


def unpack_kernel(k_ref, own, oth, f_own, f_oth):
    k = k_ref[0]
    even = k == 0
    lane = lax.broadcasted_iota(jnp.int32, (16, 128), 1)
    for j in range(16):
        for dst, half in ((f_own, k), (f_oth, 1 - k)):
            parts = []
            for m in range(4):
                at = pl.multiple_of((half * 32 + 2 * j + m // 2) * 16, 16)
                x, y = own[pl.ds(at, 16), :], oth[pl.ds(at, 16), :]
                parts.append(jnp.where(even, x, y) if m % 2 == 0 else jnp.where(even, y, x))
            for q in range(4):
                total = parts[q]
                for m in range(4):
                    if m != q:
                        moved = pltpu.roll(parts[m], (32 * (m - q)) % 128, 1)
                        total = jnp.where((lane >= 32 * m) & (lane < 32 * m + 32), moved, total)
                dst[16 * q : 16 * q + 16, 128 * j : 128 * j + 128] = total


def gather_factors(k, f):
    lines = call(pack_kernel, "pack_factors", [], [f.T], [((PEERS * 16, 128), F32)])[0]
    own = swap_chips(lines)
    oth = other_core(own)
    return call(unpack_kernel, "unpack_factors", [k], [own, oth], [((RANK, HALF), F32)] * 2)


def swap_chips(lines):
    shape = lines.shape
    parts = lines.reshape(PEERS, 1, -1)
    return lax.all_to_all(parts, CHIPS, 0, 0, tiled=True).reshape(shape)


def other_core(x):
    return lax.ppermute(x, CORE, [(0, 1), (1, 0)])


def body(panel, treat_start, loading_init, factor_init, unit_init, day_init):
    core = lax.axis_index(CORE)
    device = 2 * lax.axis_index(CHIPS) + core
    in_own = (device >> 6) == core
    k = jnp.stack([core, in_own.astype(jnp.int32), (device & 63) >> 2, device & 3]).astype(jnp.int32)
    f_own, f_oth = gather_factors(k, factor_init)
    loading = loading_init
    a = unit_init.reshape(1, ROWS)
    ts = treat_start.reshape(1, ROWS)
    b = day_init.reshape(1, DAYS)
    for _ in range(SWEEPS):
        sent, dhi_oth, dlo_oth, *rest = first_other(k, panel, f_oth, b, loading, a, ts)
        arrived = other_core(sent)
        kept, dhi_own, dlo_own, rm = first_own(k, panel, f_own, b, loading, a, ts, *rest)
        summed = sum_and_copy(swap_chips(kept + arrived))
        own = swap_chips(summed)
        oth = other_core(own)
        ginv = gram_inverse(own)
        f_own, f_oth, b, loading, a, shard = second(
            k, own, oth, ginv, f_own, f_oth, b, dhi_own, dlo_own, dhi_oth, dlo_oth, loading, a, rm
        )
    return (loading, shard.T, a.reshape(ROWS), b.reshape(DAYS))


def solution(mesh):
    finer = Mesh(
        mesh.devices.reshape(mesh.shape["gx"], mesh.shape["gy"], 4, 2), ("gx", "gy", "gz_0", "gz_1")
    )
    return jax.shard_map(
        body,
        mesh=finer,
        in_specs=(
            P(GX_GY_GZ, None),
            P(GX_GY_GZ),
            P(None, GX_GY_GZ),
            P(None, GX_GY_GZ),
            P(GX_GY_GZ),
            P(),
        ),
        out_specs=(P(None, GX_GY_GZ), P(None, GX_GY_GZ), P(GX_GY_GZ), P()),
        check_vma=False,
    )
```

```python
import functools

import jax
import jax.numpy as jnp
from jax import lax
from jax.experimental import pallas as pl
from jax.experimental.pallas import tpu as pltpu
from jax.sharding import Mesh
from jax.sharding import PartitionSpec as P

SWEEPS = 2
RIDGE = 1.0
GX_GY_GZ = ("gx", "gy", "gz_0", "gz_1")
CHIPS = ("gx", "gy", "gz_0")
CORE = "gz_1"

RANK = 64
ROWS = 256
DAYS = 4096
HALF = 2048
UNITS = 32768
BLK = 512
NBLK = HALF // BLK
PEERS = 64
CHUNK = 17
BROWS = 16 * CHUNK
PAY = PEERS * CHUNK
F32 = jnp.float32
BF = jnp.bfloat16


def dot(x, y, dims=((1,), (0,))):
    return lax.dot_general(x, y, (dims, ((), ())), preferred_element_type=F32)


def dot_exact(x, y, dims=((1,), (0,))):
    return lax.dot_general(x, y, (dims, ((), ())), preferred_element_type=F32, precision=lax.Precision.HIGHEST)


def split(x):
    hi = x.astype(BF)
    return hi, (x - hi.astype(F32)).astype(BF)


def split_rows(x):
    hi = x.astype(BF).astype(F32)
    mid = (x - hi).astype(BF).astype(F32)
    return [hi, mid, x - hi - mid]


def square_inverse(p):
    (a, b), (c, d) = p
    q = 1.0 / (a * d - b * c)
    return [[d * q, -b * q], [-c * q, a * q]]


def mul(x, y):
    return [[x[i][0] * y[0][j] + x[i][1] * y[1][j] for j in range(2)] for i in range(2)]


def block_inverse(p):
    a, b, c, d = [[[p[i + r][j + t] for t in range(2)] for r in range(2)] for i in (0, 2) for j in (0, 2)]
    ai = square_inverse(a)
    ca = mul(c, ai)
    cab = mul(ca, b)
    s = square_inverse([[d[i][j] - cab[i][j] for j in range(2)] for i in range(2)])
    ab = mul(ai, b)
    abs_ = mul(ab, s)
    corner = mul(abs_, ca)
    sca = mul(s, ca)
    top = [[ai[i][0] + corner[i][0], ai[i][1] + corner[i][1], -abs_[i][0], -abs_[i][1]] for i in range(2)]
    return top + [[-sca[i][0], -sca[i][1], s[i][0], s[i][1]] for i in range(2)]


def inverse(m, between=None):
    n = m.shape[0]
    row = lax.broadcasted_iota(jnp.int32, (n, n), 0)
    col = lax.broadcasted_iota(jnp.int32, (n, n), 1)
    w = jnp.concatenate([m, (row == col).astype(F32)], axis=1)
    w = [w[8 * t : 8 * t + 8] for t in range(n // 8)]
    rows = lax.broadcasted_iota(jnp.int32, (8, 2 * n), 0)
    for k in range(0, n, 4):
        at, r0 = k // 8, k % 8
        c = [[jnp.broadcast_to(v[:, k + j : k + j + 1], (8, 2 * n)) for j in range(4)] for v in w]
        lines = [w[at][r0 + i : r0 + i + 1] for i in range(4)]
        p = block_inverse([[c[at][j][r0 + i : r0 + i + 1] for j in range(4)] for i in range(4)])
        t = [p[i][0] * lines[0] + p[i][1] * lines[1] + (p[i][2] * lines[2] + p[i][3] * lines[3]) for i in range(4)]
        for g in range(n // 8):
            w[g] = w[g] - ((c[g][0] * t[0] + c[g][1] * t[1]) + (c[g][2] * t[2] + c[g][3] * t[3]))
        for i in range(4):
            w[at] = jnp.where(rows == r0 + i, t[i], w[at])
        if between is not None:
            between(k // 4)
    return jnp.concatenate(w, axis=0)[:, n:]


def spread(lv, av, lt, lw, gp):
    lhi, llo = split(lv)
    hi32, lo32 = lhi.astype(F32), llo.astype(F32)
    ones = jnp.ones((3, ROWS), F32)
    k_rows = [hi32, hi32, lo32] + split_rows(av) + [ones, jnp.zeros((58, ROWS), F32)]
    lt[...] = jnp.concatenate(k_rows, axis=0).T.astype(BF)
    lw[0:64] = lhi
    lw[64:128] = llo
    lw[128:144] = jnp.ones((16, ROWS), BF)
    last = ((1,), (1,))
    both = jnp.concatenate([lhi, llo], axis=0)
    g = dot(both, lhi, last)
    g = g[0:64] + g[64:128] + dot(lhi, llo, last)
    gp[0:32] = jnp.concatenate([g[0:32], g[32:64]], axis=1)
    l1 = dot(jnp.ones((16, ROWS), BF), both, last)[0:1]
    gp[32:33] = jnp.concatenate([l1[:, 0:64] + l1[:, 64:128], jnp.zeros((1, 64), F32)], axis=1)


SPREAD = [((ROWS, 256), BF), ((144, ROWS), BF), ((40, 128), F32)]


def prep_kernel(panel, b, l, a, ts, panel_out, b_out, l_out, a_out, tsb, lt, lw, gp, ts_in, sems):
    pairs = ((panel, panel_out), (b, b_out), (l, l_out), (a, a_out), (ts, ts_in))
    moves = [pltpu.make_async_copy(src, dst, sems.at[i]) for i, (src, dst) in enumerate(pairs)]
    for move in moves:
        move.start()
    for move in moves[1:]:
        move.wait()
    tsb[...] = jnp.broadcast_to(ts_in[...].astype(F32), (128, ROWS)).T
    spread(l_out[...], a_out[...], lt, lw, gp)
    moves[0].wait()


def prep(*operands):
    outs = [((ROWS, DAYS), F32), ((1, DAYS), F32), ((RANK, ROWS), F32), ((1, ROWS), F32), ((ROWS, 128), F32)] + SPREAD
    return pl.pallas_call(
        prep_kernel,
        in_specs=[pl.BlockSpec(memory_space=pltpu.HBM)] * 5,
        out_specs=[vmem()] * len(outs),
        out_shape=[pltpu.VMEM(shape, dtype) for shape, dtype in outs],
        scratch_shapes=[pltpu.VMEM((1, ROWS), jnp.int32), pltpu.SemaphoreType.DMA((5,))],
        compiler_params=pltpu.CompilerParams(vmem_limit_bytes=16 << 20),
        name="prep",
    )(*[pltpu.with_memory_space_constraint(x, pltpu.HBM) for x in operands])


def first_kernel(k_ref, panel, f, b, a, tsb, lt, lw, gp, *rest, own):
    if own:
        l, acc_in, out, dhi, dlo, rm = rest
    else:
        out, dhi, dlo, acc_out = rest
    k = k_ref[0]
    half = k if own else 1 - k
    start = pl.multiple_of(half * HALF, HALF)
    lane = lax.broadcasted_iota(jnp.int32, (ROWS, 128), 1)
    left = tsb[...] - (lane + start).astype(F32)
    run = acc_in[...] if own else jnp.zeros((ROWS, 128), F32)
    a_sum = jnp.broadcast_to(jnp.sum(a[...], axis=1, keepdims=True), (1, 128))
    for j in range(NBLK):
        whole = slice(BLK * j, BLK * (j + 1))
        fhi, flo = split(f[:, whole])
        bv = b[:, pl.ds(start + BLK * j, BLK)]
        aux = jnp.concatenate([jnp.ones((3, BLK), F32)] + split_rows(bv) + [jnp.zeros((58, BLK), F32)], axis=0)
        fa = jnp.concatenate([fhi, flo, fhi, aux.astype(BF)], axis=0)
        s = dot(lt[...], fa)
        for q in range(BLK // 128):
            at = BLK * j + 128 * q
            cols = slice(at, at + 128)
            x = panel[:, pl.ds(start + at, 128)]
            d = jnp.where(left > float(at), x - s[:, 128 * q : 128 * (q + 1)], 0.0)
            hi, lo = split(d)
            dhi[:, cols] = hi
            dlo[:, cols] = lo
            run = run + d
        r1 = dot(lw[...], dhi[:, whole])
        r2 = dot(lw[...], dlo[:, whole])
        w = r1[0:64] + r1[64:128] + r2[0:64]
        day_sum = r1[128:129] + r2[128:129]
        extra = [day_sum[:, 128 * q : 128 * (q + 1)] for q in range(4)]
        line = gp[32:33, :]
        if own and j == NBLK - 1:
            means = dot_exact(jnp.ones((8, 128), F32), run, ((1,), (1,))) * (1.0 / DAYS)
            rm[...] = means[0:1]
            lr = dot_exact(means, l[...], ((1,), (1,)))[0:1]
            line = jnp.concatenate([line[:, 0:64], lr], axis=1)
        extra += [gp[8 * j : 8 * j + 8], line, a_sum, jnp.zeros((2, 128), F32)]
        extra = jnp.concatenate(extra, axis=0)
        for i in range(8):
            for t in range(2):
                at = BROWS * j + CHUNK * (2 * i + t)
                out[at : at + 8, :] = w[8 * i : 8 * i + 8, 256 * t : 256 * t + 128]
                out[at + 8 : at + 16, :] = w[8 * i : 8 * i + 8, 256 * t + 128 : 256 * t + 256]
                out[at + 16 : at + 17, :] = extra[2 * i + t : 2 * i + t + 1]
    if not own:
        acc_out[...] = run


def vmem():
    return pl.BlockSpec(memory_space=pltpu.VMEM)


def smem():
    return pl.BlockSpec(memory_space=pltpu.SMEM)


def call(kernel, name, scalars, operands, outs, scratch=(), place=pltpu.VMEM):
    return pl.pallas_call(
        kernel,
        in_specs=[smem()] * len(scalars) + [vmem()] * len(operands),
        out_specs=[vmem()] * len(outs),
        out_shape=[place(shape, dtype) for shape, dtype in outs],
        scratch_shapes=list(scratch),
        compiler_params=pltpu.CompilerParams(vmem_limit_bytes=16 << 20),
        name=name,
    )(*scalars, *[pltpu.with_memory_space_constraint(x, pltpu.VMEM) for x in operands])


def first_other(k, panel, f, b, a, *spreads):
    outs = [((PAY, 128), F32), ((ROWS, HALF), BF), ((ROWS, HALF), BF), ((ROWS, 128), F32)]
    return call(functools.partial(first_kernel, own=False), "first_other", [k], [panel, f, b, a, *spreads], outs)


def first_own(k, panel, f, b, a, *rest):
    outs = [((PAY, 128), F32), ((ROWS, HALF), BF), ((ROWS, HALF), BF), ((1, ROWS), F32)]
    return call(functools.partial(first_kernel, own=True), "first_own", [k], [panel, f, b, a, *rest], outs)


def sum_kernel(x, out):
    slab = x[0 : 8 * CHUNK, :]
    for g in range(1, 8):
        slab = slab + x[8 * CHUNK * g : 8 * CHUNK * (g + 1), :]
    total = slab[0:CHUNK]
    for c in range(1, 8):
        total = total + slab[CHUNK * c : CHUNK * (c + 1)]
    slab = jnp.concatenate([total] * 8, axis=0)
    for g in range(8):
        out[8 * CHUNK * g : 8 * CHUNK * (g + 1), :] = slab


def sum_and_copy(x):
    return call(sum_kernel, "sum_and_copy", [], [x], [((PAY, 128), F32)])[0]


def extra_row(x, j, e):
    at = BROWS * j + CHUNK * e + 16
    return x[at : at + 1, :]


def gram_kernel(x, out):
    packed = jnp.concatenate([extra_row(x, j, 4 + e) for j in range(4) for e in range(8)], axis=0)
    g = jnp.concatenate([packed[:, 0:64], packed[:, 64:128]], axis=0)
    row = lax.broadcasted_iota(jnp.int32, (RANK, RANK), 0)
    col = lax.broadcasted_iota(jnp.int32, (RANK, RANK), 1)
    out[...] = inverse(g + jnp.where(row == col, RIDGE, 0.0))


def gram_inverse(x):
    return call(gram_kernel, "gram_inverse", [], [x], [((RANK, RANK), F32)])[0]


def second_kernel(k_ref, own, oth, ginv, f_own, f_oth, b_ref, dhi_own, dlo_own, dhi_oth, dlo_oth, l, a, rm, *rest, final):
    if final:
        bn, ln, an, shard, fn_own, fn_oth, bt, turn = rest
    else:
        bn, ln, an, fn_own, fn_oth, lt, lw, gp, bt = rest
    k = k_ref[0]
    starts = [pl.multiple_of(k * HALF, HALF), pl.multiple_of((1 - k) * HALF, HALF)]
    sums = [jnp.concatenate([extra_row(x, j, q) for j in range(4) for q in range(4)], axis=1) for x in (own, oth)]
    mean_d = jnp.sum(sums[0] + sums[1], axis=1, keepdims=True) * (1.0 / (UNITS * DAYS))
    mean_b = jnp.sum(b_ref[...], axis=1, keepdims=True) * (1.0 / DAYS)
    mean_a = extra_row(own, 3, 13)[:, 0:1] * (1.0 / UNITS)
    lane = lax.broadcasted_iota(jnp.int32, (1, 128), 1)
    l_own, l_oth = extra_row(own, 3, 12), extra_row(oth, 3, 12)
    lines = l_own + jnp.where(lane >= 64, l_oth, 0.0)
    turned = jnp.broadcast_to(lines, (128, 128)).T
    l1 = turned[0:64, 0:1]
    u = (mean_d + mean_a) * l1 - turned[64:128, 0:1]
    ghi, glo = split(ginv[...])
    gcat = jnp.concatenate([ghi, ghi, glo], axis=1)
    hx = jnp.zeros((2 * RANK, 2 * RANK), F32)
    hl = jnp.zeros((2 * RANK, RANK), F32)
    f1 = jnp.zeros((RANK, 128), F32)
    fb = jnp.zeros((RANK, 128), F32)
    for side, (x, f, fn, col, start) in enumerate(
        ((own, f_own, fn_own, sums[0], starts[0]), (oth, f_oth, fn_oth, sums[1], starts[1]))
    ):
        v = mean_d + mean_b - col * (1.0 / UNITS)
        bn[:, pl.ds(start, HALF)] = b_ref[:, pl.ds(start, HALF)] - v
        for j in range(NBLK):
            cols = slice(BLK * j, BLK * (j + 1))
            lines = []
            for i in range(8):
                tiles = []
                for t in range(2):
                    at = BROWS * j + CHUNK * (2 * i + t)
                    tiles += [x[at : at + 8, :], x[at + 8 : at + 16, :]]
                lines.append(jnp.concatenate(tiles, axis=1))
            w = jnp.concatenate(lines, axis=0)
            fv = f[:, cols]
            vb = v[:, cols]
            r = w + u + l1 * vb - fv
            rhi, rlo = split(r)
            new = fv + dot(gcat, jnp.concatenate([rhi, rlo, rhi], axis=0))
            fn[:, cols] = new
            nhi, nlo = split(new)
            ohi, olo = split(fv)
            both = jnp.concatenate([nhi, nlo], axis=0).T
            bt[HALF * side + BLK * j : HALF * side + BLK * (j + 1), :] = both
            hx = hx + dot(jnp.concatenate([nhi, ohi], axis=0), both)
            hl = hl + dot(jnp.concatenate([nlo, olo], axis=0), both[:, 0:64])
            nb = new * vb
            for q in range(BLK // 128):
                f1 = f1 + new[:, 128 * q : 128 * (q + 1)]
                fb = fb + nb[:, 128 * q : 128 * (q + 1)]
    f1 = jnp.sum(f1, axis=1, keepdims=True)
    fb = jnp.sum(fb, axis=1, keepdims=True)
    da = mean_d + mean_a - rm[...]
    a_new = a[...] - da
    an[...] = a_new
    row = lax.broadcasted_iota(jnp.int32, (RANK, RANK), 0)
    col = lax.broadcasted_iota(jnp.int32, (RANK, RANK), 1)
    h = hx[0:64, 0:64] + hx[0:64, 64:128] + hl[0:64]
    xt = hx[64:128, 0:64] + hx[64:128, 64:128] + hl[64:128]
    zs = []

    def product(step):
        if step % 2 == 0:
            at = 512 * (step // 2)
            hi, lo = (dhi_own, dlo_own) if at < HALF else (dhi_oth, dlo_oth)
            inner = slice(at % HALF, at % HALF + 512)
            z = dot(hi[:, inner], bt[at : at + 512, :])
            zs.append(z[:, 0:64] + z[:, 64:128] + dot(lo[:, inner], bt[at : at + 512, 0:64]))

    hinv = inverse(h + jnp.where(row == col, RIDGE, 0.0), product)
    zt = zs[0]
    for z in zs[1:]:
        zt = zt + z
    p = dot_exact(xt, l[...], ((0,), (0,))) + f1 * da + fb + zt.T
    l_new = dot_exact(hinv, p)
    ln[...] = l_new
    if final:
        tile = pl.multiple_of(128 * k_ref[2], 128)
        mine = jnp.where(k_ref[1] == 1, fn_own[:, pl.ds(tile, 128)], fn_oth[:, pl.ds(tile, 128)])
        turn[...] = mine.T
        shard[...] = turn[pl.ds(pl.multiple_of(32 * k_ref[3], 32), 32), :]
    else:
        spread(l_new, a_new, lt, lw, gp)


def second(k, final, *operands):
    outs = [((1, DAYS), F32), ((RANK, ROWS), F32), ((1, ROWS), F32)]
    kernel = functools.partial(second_kernel, final=final)
    half = ((RANK, HALF), F32)
    turned = pltpu.VMEM((DAYS, 128), BF)
    if final:
        scratch = [pltpu.VMEM(*half), pltpu.VMEM(*half), turned, pltpu.VMEM((128, RANK), F32)]
        outs = outs + [((32, RANK), F32)]
        return call(kernel, "second_last", [k], operands, outs, scratch, jax.ShapeDtypeStruct)
    return call(kernel, "second", [k], operands, outs + [half, half] + SPREAD, [turned])


def pack_kernel(x, out):
    v = x[...].T
    packed = jnp.concatenate([v[16 * q : 16 * q + 16] for q in range(4)], axis=1)
    for c in range(PEERS):
        out[16 * c : 16 * c + 16, :] = packed


def unpack_kernel(k_ref, own, oth, f_own, f_oth):
    k = k_ref[0]
    even = k == 0
    lane = lax.broadcasted_iota(jnp.int32, (16, 128), 1)
    for j in range(16):
        for dst, half in ((f_own, k), (f_oth, 1 - k)):
            parts = []
            for m in range(4):
                at = pl.multiple_of((half * 32 + 2 * j + m // 2) * 16, 16)
                x, y = own[pl.ds(at, 16), :], oth[pl.ds(at, 16), :]
                parts.append(jnp.where(even, x, y) if m % 2 == 0 else jnp.where(even, y, x))
            for q in range(4):
                total = parts[q]
                for m in range(4):
                    if m != q:
                        moved = pltpu.roll(parts[m], (32 * (m - q)) % 128, 1)
                        total = jnp.where((lane >= 32 * m) & (lane < 32 * m + 32), moved, total)
                dst[16 * q : 16 * q + 16, 128 * j : 128 * j + 128] = total


def gather_factors(k, f):
    lines = call(pack_kernel, "pack_factors", [], [f.T], [((PEERS * 16, 128), F32)])[0]
    own = swap_chips(lines)
    oth = other_core(own)
    return call(unpack_kernel, "unpack_factors", [k], [own, oth], [((RANK, HALF), F32)] * 2)


def swap_chips(lines):
    shape = lines.shape
    parts = lines.reshape(PEERS, 1, -1)
    return lax.all_to_all(parts, CHIPS, 0, 0, tiled=True).reshape(shape)


def other_core(x):
    return lax.ppermute(x, CORE, [(0, 1), (1, 0)])


def body(panel, treat_start, loading_init, factor_init, unit_init, day_init):
    core = lax.axis_index(CORE)
    device = 2 * lax.axis_index(CHIPS) + core
    in_own = (device >> 6) == core
    k = jnp.stack([core, in_own.astype(jnp.int32), (device & 63) >> 2, device & 3]).astype(jnp.int32)
    f_own, f_oth = gather_factors(k, factor_init)
    ts = treat_start.reshape(1, ROWS)
    panel, b, loading, a, tsb, *spreads = prep(
        panel, day_init.reshape(1, DAYS), loading_init, unit_init.reshape(1, ROWS), ts
    )
    for sweep in range(SWEEPS):
        sent, dhi_oth, dlo_oth, acc = first_other(k, panel, f_oth, b, a, tsb, *spreads)
        arrived = other_core(sent)
        kept, dhi_own, dlo_own, rm = first_own(k, panel, f_own, b, a, tsb, *spreads, loading, acc)
        summed = sum_and_copy(swap_chips(kept + arrived))
        own = swap_chips(summed)
        oth = other_core(own)
        ginv = gram_inverse(own)
        final = sweep == SWEEPS - 1
        b, loading, a, *rest = second(
            k, final, own, oth, ginv, f_own, f_oth, b, dhi_own, dlo_own, dhi_oth, dlo_oth, loading, a, rm
        )
        if not final:
            f_own, f_oth, *spreads = rest
    return (loading, rest[0].T, a.reshape(ROWS), b.reshape(DAYS))


def solution(mesh):
    finer = Mesh(
        mesh.devices.reshape(mesh.shape["gx"], mesh.shape["gy"], 4, 2), ("gx", "gy", "gz_0", "gz_1")
    )
    return jax.shard_map(
        body,
        mesh=finer,
        in_specs=(
            P(GX_GY_GZ, None),
            P(GX_GY_GZ),
            P(None, GX_GY_GZ),
            P(None, GX_GY_GZ),
            P(GX_GY_GZ),
            P(),
        ),
        out_specs=(P(None, GX_GY_GZ), P(None, GX_GY_GZ), P(GX_GY_GZ), P()),
        check_vma=False,
    )
```

```python
import functools

import jax
import jax.numpy as jnp
from jax import lax
from jax.experimental import pallas as pl
from jax.experimental.pallas import tpu as pltpu
from jax.sharding import Mesh
from jax.sharding import PartitionSpec as P

SWEEPS = 2
RIDGE = 1.0
GX_GY_GZ = ("gx", "gy", "gz_0", "gz_1")
CHIPS = ("gx", "gy", "gz_0")
CORE = "gz_1"

RANK = 64
ROWS = 256
DAYS = 4096
HALF = 2048
UNITS = 32768
BLK = 512
NBLK = HALF // BLK
PEERS = 64
CHUNK = 17
BROWS = 16 * CHUNK
PAY = PEERS * CHUNK
F32 = jnp.float32
BF = jnp.bfloat16


def dot(x, y, dims=((1,), (0,))):
    return lax.dot_general(x, y, (dims, ((), ())), preferred_element_type=F32)


def dot_exact(x, y, dims=((1,), (0,))):
    return lax.dot_general(x, y, (dims, ((), ())), preferred_element_type=F32, precision=lax.Precision.HIGHEST)


def split(x):
    hi = x.astype(BF)
    return hi, (x - hi.astype(F32)).astype(BF)


def split_rows(x):
    hi = x.astype(BF).astype(F32)
    mid = (x - hi).astype(BF).astype(F32)
    return [hi, mid, x - hi - mid]


def square_inverse(p):
    (a, b), (c, d) = p
    q = 1.0 / (a * d - b * c)
    return [[d * q, -b * q], [-c * q, a * q]]


def mul(x, y):
    return [[x[i][0] * y[0][j] + x[i][1] * y[1][j] for j in range(2)] for i in range(2)]


def block_inverse(p):
    a, b, c, d = [[[p[i + r][j + t] for t in range(2)] for r in range(2)] for i in (0, 2) for j in (0, 2)]
    ai = square_inverse(a)
    ca = mul(c, ai)
    cab = mul(ca, b)
    s = square_inverse([[d[i][j] - cab[i][j] for j in range(2)] for i in range(2)])
    ab = mul(ai, b)
    abs_ = mul(ab, s)
    corner = mul(abs_, ca)
    sca = mul(s, ca)
    top = [[ai[i][0] + corner[i][0], ai[i][1] + corner[i][1], -abs_[i][0], -abs_[i][1]] for i in range(2)]
    return top + [[-sca[i][0], -sca[i][1], s[i][0], s[i][1]] for i in range(2)]


def inverse(m, between=None):
    n = m.shape[0]
    row = lax.broadcasted_iota(jnp.int32, (n, n), 0)
    col = lax.broadcasted_iota(jnp.int32, (n, n), 1)
    w = jnp.concatenate([m, (row == col).astype(F32)], axis=1)
    w = [w[8 * t : 8 * t + 8] for t in range(n // 8)]
    rows = lax.broadcasted_iota(jnp.int32, (8, 2 * n), 0)
    for k in range(0, n, 4):
        at, r0 = k // 8, k % 8
        c = [[jnp.broadcast_to(v[:, k + j : k + j + 1], (8, 2 * n)) for j in range(4)] for v in w]
        lines = [w[at][r0 + i : r0 + i + 1] for i in range(4)]
        p = block_inverse([[c[at][j][r0 + i : r0 + i + 1] for j in range(4)] for i in range(4)])
        t = [p[i][0] * lines[0] + p[i][1] * lines[1] + (p[i][2] * lines[2] + p[i][3] * lines[3]) for i in range(4)]
        for g in range(n // 8):
            w[g] = w[g] - ((c[g][0] * t[0] + c[g][1] * t[1]) + (c[g][2] * t[2] + c[g][3] * t[3]))
        for i in range(4):
            w[at] = jnp.where(rows == r0 + i, t[i], w[at])
        if between is not None:
            between(k // 4)
    return jnp.concatenate(w, axis=0)[:, n:]


def spread(lv, av, lt, lw, gp):
    lhi, llo = split(lv)
    hi32, lo32 = lhi.astype(F32), llo.astype(F32)
    ones = jnp.ones((3, ROWS), F32)
    k_rows = [hi32, hi32, lo32] + split_rows(av) + [ones, jnp.zeros((58, ROWS), F32)]
    lt[...] = jnp.concatenate(k_rows, axis=0).T.astype(BF)
    lw[0:64] = lhi
    lw[64:128] = llo
    lw[128:144] = jnp.ones((16, ROWS), BF)
    last = ((1,), (1,))
    both = jnp.concatenate([lhi, llo], axis=0)
    g = dot(both, lhi, last)
    g = g[0:64] + g[64:128] + dot(lhi, llo, last)
    gp[0:32] = jnp.concatenate([g[0:32], g[32:64]], axis=1)
    l1 = dot(jnp.ones((16, ROWS), BF), both, last)[0:1]
    gp[32:33] = jnp.concatenate([l1[:, 0:64] + l1[:, 64:128], jnp.zeros((1, 64), F32)], axis=1)


SPREAD = [((ROWS, 256), BF), ((144, ROWS), BF), ((40, 128), F32)]


def prep_kernel(panel, b, l, a, ts, panel_out, b_out, l_out, a_out, tsb, lt, lw, gp, ts_in, sems):
    pairs = ((panel, panel_out), (b, b_out), (l, l_out), (a, a_out), (ts, ts_in))
    moves = [pltpu.make_async_copy(src, dst, sems.at[i]) for i, (src, dst) in enumerate(pairs)]
    for move in moves:
        move.start()
    for move in moves[1:]:
        move.wait()
    tsb[...] = jnp.broadcast_to(ts_in[...].astype(F32), (128, ROWS)).T
    spread(l_out[...], a_out[...], lt, lw, gp)
    moves[0].wait()


def prep(*operands):
    outs = [((ROWS, DAYS), F32), ((1, DAYS), F32), ((RANK, ROWS), F32), ((1, ROWS), F32), ((ROWS, 128), F32)] + SPREAD
    return pl.pallas_call(
        prep_kernel,
        in_specs=[pl.BlockSpec(memory_space=pltpu.HBM)] * 5,
        out_specs=[vmem()] * len(outs),
        out_shape=[pltpu.VMEM(shape, dtype) for shape, dtype in outs],
        scratch_shapes=[pltpu.VMEM((1, ROWS), jnp.int32), pltpu.SemaphoreType.DMA((5,))],
        compiler_params=pltpu.CompilerParams(vmem_limit_bytes=16 << 20),
        name="prep",
    )(*[pltpu.with_memory_space_constraint(x, pltpu.HBM) for x in operands])


def first_kernel(k_ref, panel, f, b, a, tsb, lt, lw, gp, *rest, own):
    if own:
        l, acc_in, out, dhi, dlo, rm = rest
    else:
        out, dhi, dlo, acc_out = rest
    k = k_ref[0]
    half = k if own else 1 - k
    start = pl.multiple_of(half * HALF, HALF)
    lane = lax.broadcasted_iota(jnp.int32, (ROWS, 128), 1)
    left = tsb[...] - (lane + start).astype(F32)
    run = acc_in[...] if own else jnp.zeros((ROWS, 128), F32)
    a_sum = jnp.broadcast_to(jnp.sum(a[...], axis=1, keepdims=True), (1, 128))

    def fit(j):
        fhi, flo = split(f[:, BLK * j : BLK * (j + 1)])
        bv = b[:, pl.ds(start + BLK * j, BLK)]
        aux = jnp.concatenate([jnp.ones((3, BLK), F32)] + split_rows(bv) + [jnp.zeros((58, BLK), F32)], axis=0)
        return dot(lt[...], jnp.concatenate([fhi, flo, fhi, aux.astype(BF)], axis=0))

    def weigh(j):
        whole = slice(BLK * j, BLK * (j + 1))
        r1 = dot(lw[...], dhi[:, whole])
        r2 = dot(lw[...], dlo[:, whole])
        w = r1[0:64] + r1[64:128] + r2[0:64]
        day_sum = r1[128:129] + r2[128:129]
        extra = [day_sum[:, 128 * q : 128 * (q + 1)] for q in range(4)]
        line = gp[32:33, :]
        if own and j == NBLK - 1:
            means = dot_exact(jnp.ones((8, 128), F32), run, ((1,), (1,))) * (1.0 / DAYS)
            rm[...] = means[0:1]
            lr = dot_exact(means, l[...], ((1,), (1,)))[0:1]
            line = jnp.concatenate([line[:, 0:64], lr], axis=1)
        extra += [gp[8 * j : 8 * j + 8], line, a_sum, jnp.zeros((2, 128), F32)]
        extra = jnp.concatenate(extra, axis=0)
        for i in range(8):
            for t in range(2):
                at = BROWS * j + CHUNK * (2 * i + t)
                out[at : at + 8, :] = w[8 * i : 8 * i + 8, 256 * t : 256 * t + 128]
                out[at + 8 : at + 16, :] = w[8 * i : 8 * i + 8, 256 * t + 128 : 256 * t + 256]
                out[at + 16 : at + 17, :] = extra[2 * i + t : 2 * i + t + 1]

    s = fit(0)
    for j in range(NBLK):
        following = fit(j + 1) if j + 1 < NBLK else None
        for q in range(BLK // 128):
            at = BLK * j + 128 * q
            cols = slice(at, at + 128)
            x = panel[:, pl.ds(start + at, 128)]
            d = jnp.where(left > float(at), x - s[:, 128 * q : 128 * (q + 1)], 0.0)
            hi, lo = split(d)
            dhi[:, cols] = hi
            dlo[:, cols] = lo
            run = run + d
        s = following
        if j:
            weigh(j - 1)
    weigh(NBLK - 1)
    if not own:
        acc_out[...] = run


def vmem():
    return pl.BlockSpec(memory_space=pltpu.VMEM)


def smem():
    return pl.BlockSpec(memory_space=pltpu.SMEM)


def call(kernel, name, scalars, operands, outs, scratch=(), place=pltpu.VMEM):
    return pl.pallas_call(
        kernel,
        in_specs=[smem()] * len(scalars) + [vmem()] * len(operands),
        out_specs=[vmem()] * len(outs),
        out_shape=[place(shape, dtype) for shape, dtype in outs],
        scratch_shapes=list(scratch),
        compiler_params=pltpu.CompilerParams(vmem_limit_bytes=16 << 20),
        name=name,
    )(*scalars, *[pltpu.with_memory_space_constraint(x, pltpu.VMEM) for x in operands])


def first_other(k, panel, f, b, a, *spreads):
    outs = [((PAY, 128), F32), ((ROWS, HALF), BF), ((ROWS, HALF), BF), ((ROWS, 128), F32)]
    return call(functools.partial(first_kernel, own=False), "first_other", [k], [panel, f, b, a, *spreads], outs)


def first_own(k, panel, f, b, a, *rest):
    outs = [((PAY, 128), F32), ((ROWS, HALF), BF), ((ROWS, HALF), BF), ((1, ROWS), F32)]
    return call(functools.partial(first_kernel, own=True), "first_own", [k], [panel, f, b, a, *rest], outs)


def sum_kernel(x, out):
    slab = x[0 : 8 * CHUNK, :]
    for g in range(1, 8):
        slab = slab + x[8 * CHUNK * g : 8 * CHUNK * (g + 1), :]
    total = slab[0:CHUNK]
    for c in range(1, 8):
        total = total + slab[CHUNK * c : CHUNK * (c + 1)]
    slab = jnp.concatenate([total] * 8, axis=0)
    for g in range(8):
        out[8 * CHUNK * g : 8 * CHUNK * (g + 1), :] = slab


def sum_and_copy(x):
    return call(sum_kernel, "sum_and_copy", [], [x], [((PAY, 128), F32)])[0]


def extra_row(x, j, e):
    at = BROWS * j + CHUNK * e + 16
    return x[at : at + 1, :]


def gram_kernel(x, out):
    packed = jnp.concatenate([extra_row(x, j, 4 + e) for j in range(4) for e in range(8)], axis=0)
    g = jnp.concatenate([packed[:, 0:64], packed[:, 64:128]], axis=0)
    row = lax.broadcasted_iota(jnp.int32, (RANK, RANK), 0)
    col = lax.broadcasted_iota(jnp.int32, (RANK, RANK), 1)
    out[...] = inverse(g + jnp.where(row == col, RIDGE, 0.0))


def gram_inverse(x):
    return call(gram_kernel, "gram_inverse", [], [x], [((RANK, RANK), F32)])[0]


def second_kernel(k_ref, own, oth, ginv, f_own, f_oth, b_ref, dhi_own, dlo_own, dhi_oth, dlo_oth, l, a, rm, *rest, final):
    if final:
        bn, ln, an, shard, fn_own, fn_oth, bt, his, los, turn = rest
    else:
        bn, ln, an, fn_own, fn_oth, lt, lw, gp, bt, his, los = rest
    k = k_ref[0]
    starts = [pl.multiple_of(k * HALF, HALF), pl.multiple_of((1 - k) * HALF, HALF)]
    sums = [jnp.concatenate([extra_row(x, j, q) for j in range(4) for q in range(4)], axis=1) for x in (own, oth)]
    mean_d = jnp.sum(sums[0] + sums[1], axis=1, keepdims=True) * (1.0 / (UNITS * DAYS))
    mean_b = jnp.sum(b_ref[...], axis=1, keepdims=True) * (1.0 / DAYS)
    mean_a = extra_row(own, 3, 13)[:, 0:1] * (1.0 / UNITS)
    lane = lax.broadcasted_iota(jnp.int32, (1, 128), 1)
    l_own, l_oth = extra_row(own, 3, 12), extra_row(oth, 3, 12)
    lines = l_own + jnp.where(lane >= 64, l_oth, 0.0)
    turned = jnp.broadcast_to(lines, (128, 128)).T
    l1 = turned[0:64, 0:1]
    u = (mean_d + mean_a) * l1 - turned[64:128, 0:1]
    ghi, glo = split(ginv[...])
    gcat = jnp.concatenate([ghi, ghi, glo], axis=1)
    f1 = jnp.zeros((RANK, 128), F32)
    fb = jnp.zeros((RANK, 128), F32)
    for side, (x, f, fn, col, start) in enumerate(
        ((own, f_own, fn_own, sums[0], starts[0]), (oth, f_oth, fn_oth, sums[1], starts[1]))
    ):
        v = mean_d + mean_b - col * (1.0 / UNITS)
        bn[:, pl.ds(start, HALF)] = b_ref[:, pl.ds(start, HALF)] - v
        def solved(j, x=x, f=f, v=v):
            cols = slice(BLK * j, BLK * (j + 1))
            lines = []
            for i in range(8):
                tiles = []
                for t in range(2):
                    at = BROWS * j + CHUNK * (2 * i + t)
                    tiles += [x[at : at + 8, :], x[at + 8 : at + 16, :]]
                lines.append(jnp.concatenate(tiles, axis=1))
            fv = f[:, cols]
            r = jnp.concatenate(lines, axis=0) + u + l1 * v[:, cols] - fv
            rhi, rlo = split(r)
            return fv, dot(gcat, jnp.concatenate([rhi, rlo, rhi], axis=0))

        pending = solved(0)
        for j in range(NBLK):
            cols = slice(BLK * j, BLK * (j + 1))
            fv, step = pending
            if j + 1 < NBLK:
                pending = solved(j + 1)
            new = fv + step
            fn[:, cols] = new
            nhi, nlo = split(new)
            ohi, olo = split(fv)
            both = jnp.concatenate([nhi, nlo], axis=0).T
            at = HALF * side + BLK * j
            bt[at : at + BLK, :] = both
            his[:, at : at + BLK] = jnp.concatenate([nhi, ohi], axis=0)
            los[:, at : at + BLK] = olo
            nb = new * v[:, cols]
            for q in range(BLK // 128):
                f1 = f1 + new[:, 128 * q : 128 * (q + 1)]
                fb = fb + nb[:, 128 * q : 128 * (q + 1)]
    hx = dot(his[...], bt[...])
    hl = dot(los[...], bt[:, 0:64])
    f1 = jnp.sum(f1, axis=1, keepdims=True)
    fb = jnp.sum(fb, axis=1, keepdims=True)
    da = mean_d + mean_a - rm[...]
    a_new = a[...] - da
    an[...] = a_new
    row = lax.broadcasted_iota(jnp.int32, (RANK, RANK), 0)
    col = lax.broadcasted_iota(jnp.int32, (RANK, RANK), 1)
    h = hx[0:64, 0:64] + hx[0:64, 64:128] + hx[0:64, 64:128].T
    xt = hx[64:128, 0:64] + hx[64:128, 64:128] + hl
    zt = jnp.zeros((ROWS, RANK), F32)
    for at, hi, lo in ((0, dhi_own, dlo_own), (HALF, dhi_oth, dlo_oth)):
        z = dot(hi[...], bt[at : at + HALF, :])
        zt = zt + z[:, 0:64] + z[:, 64:128] + dot(lo[...], bt[at : at + HALF, 0:64])
    hinv = inverse(h + jnp.where(row == col, RIDGE, 0.0))
    p = dot_exact(xt, l[...], ((0,), (0,))) + f1 * da + fb + zt.T
    l_new = dot_exact(hinv, p)
    ln[...] = l_new
    if final:
        tile = pl.multiple_of(128 * k_ref[2], 128)
        mine = jnp.where(k_ref[1] == 1, fn_own[:, pl.ds(tile, 128)], fn_oth[:, pl.ds(tile, 128)])
        turn[...] = mine.T
        shard[...] = turn[pl.ds(pl.multiple_of(32 * k_ref[3], 32), 32), :]
    else:
        spread(l_new, a_new, lt, lw, gp)


def second(k, final, *operands):
    outs = [((1, DAYS), F32), ((RANK, ROWS), F32), ((1, ROWS), F32)]
    kernel = functools.partial(second_kernel, final=final)
    half = ((RANK, HALF), F32)
    work = [pltpu.VMEM((DAYS, 128), BF), pltpu.VMEM((128, DAYS), BF), pltpu.VMEM((64, DAYS), BF)]
    if final:
        scratch = [pltpu.VMEM(*half), pltpu.VMEM(*half), *work, pltpu.VMEM((128, RANK), F32)]
        outs = outs + [((32, RANK), F32)]
        return call(kernel, "second_last", [k], operands, outs, scratch, jax.ShapeDtypeStruct)
    return call(kernel, "second", [k], operands, outs + [half, half] + SPREAD, work)


def pack_kernel(x, out):
    v = x[...].T
    packed = jnp.concatenate([v[16 * q : 16 * q + 16] for q in range(4)], axis=1)
    for c in range(PEERS):
        out[16 * c : 16 * c + 16, :] = packed


def unpack_kernel(k_ref, own, oth, f_own, f_oth):
    k = k_ref[0]
    even = k == 0
    lane = lax.broadcasted_iota(jnp.int32, (16, 128), 1)
    for j in range(16):
        for dst, half in ((f_own, k), (f_oth, 1 - k)):
            parts = []
            for m in range(4):
                at = pl.multiple_of((half * 32 + 2 * j + m // 2) * 16, 16)
                x, y = own[pl.ds(at, 16), :], oth[pl.ds(at, 16), :]
                parts.append(jnp.where(even, x, y) if m % 2 == 0 else jnp.where(even, y, x))
            for q in range(4):
                total = parts[q]
                for m in range(4):
                    if m != q:
                        moved = pltpu.roll(parts[m], (32 * (m - q)) % 128, 1)
                        total = jnp.where((lane >= 32 * m) & (lane < 32 * m + 32), moved, total)
                dst[16 * q : 16 * q + 16, 128 * j : 128 * j + 128] = total


def gather_factors(k, f):
    lines = call(pack_kernel, "pack_factors", [], [f.T], [((PEERS * 16, 128), F32)])[0]
    own = swap_chips(lines)
    oth = other_core(own)
    return call(unpack_kernel, "unpack_factors", [k], [own, oth], [((RANK, HALF), F32)] * 2)


def swap_chips(lines):
    shape = lines.shape
    parts = lines.reshape(PEERS, 1, -1)
    return lax.all_to_all(parts, CHIPS, 0, 0, tiled=True).reshape(shape)


def other_core(x):
    return lax.ppermute(x, CORE, [(0, 1), (1, 0)])


def body(panel, treat_start, loading_init, factor_init, unit_init, day_init):
    core = lax.axis_index(CORE)
    device = 2 * lax.axis_index(CHIPS) + core
    in_own = (device >> 6) == core
    k = jnp.stack([core, in_own.astype(jnp.int32), (device & 63) >> 2, device & 3]).astype(jnp.int32)
    f_own, f_oth = gather_factors(k, factor_init)
    ts = treat_start.reshape(1, ROWS)
    panel, b, loading, a, tsb, *spreads = prep(
        panel, day_init.reshape(1, DAYS), loading_init, unit_init.reshape(1, ROWS), ts
    )
    for sweep in range(SWEEPS):
        sent, dhi_oth, dlo_oth, acc = first_other(k, panel, f_oth, b, a, tsb, *spreads)
        arrived = other_core(sent)
        kept, dhi_own, dlo_own, rm = first_own(k, panel, f_own, b, a, tsb, *spreads, loading, acc)
        summed = sum_and_copy(swap_chips(kept + arrived))
        own = swap_chips(summed)
        oth = other_core(own)
        ginv = gram_inverse(own)
        final = sweep == SWEEPS - 1
        b, loading, a, *rest = second(
            k, final, own, oth, ginv, f_own, f_oth, b, dhi_own, dlo_own, dhi_oth, dlo_oth, loading, a, rm
        )
        if not final:
            f_own, f_oth, *spreads = rest
    return (loading, rest[0].T, a.reshape(ROWS), b.reshape(DAYS))


def solution(mesh):
    finer = Mesh(
        mesh.devices.reshape(mesh.shape["gx"], mesh.shape["gy"], 4, 2), ("gx", "gy", "gz_0", "gz_1")
    )
    return jax.shard_map(
        body,
        mesh=finer,
        in_specs=(
            P(GX_GY_GZ, None),
            P(GX_GY_GZ),
            P(None, GX_GY_GZ),
            P(None, GX_GY_GZ),
            P(GX_GY_GZ),
            P(),
        ),
        out_specs=(P(None, GX_GY_GZ), P(None, GX_GY_GZ), P(GX_GY_GZ), P()),
        check_vma=False,
    )
```

```python
import functools

import jax
import jax.numpy as jnp
from jax import lax
from jax.experimental import pallas as pl
from jax.experimental.pallas import tpu as pltpu
from jax.sharding import Mesh
from jax.sharding import PartitionSpec as P

SWEEPS = 2
RIDGE = 1.0
GX_GY_GZ = ("gx", "gy", "gz_0", "gz_1")
CHIPS = ("gx", "gy", "gz_0")
CORE = "gz_1"

RANK = 64
ROWS = 256
DAYS = 4096
HALF = 2048
UNITS = 32768
BLK = 512
NBLK = HALF // BLK
PEERS = 64
CHUNK = 17
BROWS = 16 * CHUNK
PAY = PEERS * CHUNK
F32 = jnp.float32
BF = jnp.bfloat16


def dot(x, y, dims=((1,), (0,))):
    return lax.dot_general(x, y, (dims, ((), ())), preferred_element_type=F32)


def dot_exact(x, y, dims=((1,), (0,))):
    return lax.dot_general(x, y, (dims, ((), ())), preferred_element_type=F32, precision=lax.Precision.HIGHEST)


def split(x):
    hi = x.astype(BF)
    return hi, (x - hi.astype(F32)).astype(BF)


def split_rows(x):
    hi = x.astype(BF).astype(F32)
    mid = (x - hi).astype(BF).astype(F32)
    return [hi, mid, x - hi - mid]


def pair_inverse(a, b, d):
    q = 1.0 / (a * d - b * b)
    return d * q, -b * q, a * q


def block_inverse(p):
    a0, a1, a2 = pair_inverse(p[0, 0], p[0, 1], p[1, 1])
    top, low = (a0, a1), (a1, a2)
    ab = [[r[0] * p[0, c] + r[1] * p[1, c] for c in (2, 3)] for r in (top, low)]
    s00 = p[2, 2] - (p[0, 2] * ab[0][0] + p[1, 2] * ab[1][0])
    s01 = p[2, 3] - (p[0, 2] * ab[0][1] + p[1, 2] * ab[1][1])
    s11 = p[3, 3] - (p[0, 3] * ab[0][1] + p[1, 3] * ab[1][1])
    s0, s1, s2 = pair_inverse(s00, s01, s11)
    k = [[-(r[0] * s0 + r[1] * s1), -(r[0] * s1 + r[1] * s2)] for r in ab]
    c00 = a0 - (k[0][0] * ab[0][0] + k[0][1] * ab[0][1])
    c01 = a1 - (k[0][0] * ab[1][0] + k[0][1] * ab[1][1])
    c11 = a2 - (k[1][0] * ab[1][0] + k[1][1] * ab[1][1])
    return [
        [c00, c01, k[0][0], k[0][1]],
        [c01, c11, k[1][0], k[1][1]],
        [k[0][0], k[1][0], s0, s1],
        [k[0][1], k[1][1], s1, s2],
    ]


def inverse(m):
    n = m.shape[0]
    row = lax.broadcasted_iota(jnp.int32, (n, n), 0)
    col = lax.broadcasted_iota(jnp.int32, (n, n), 1)
    w = jnp.concatenate([m, (row == col).astype(F32)], axis=1)
    w = [w[8 * t : 8 * t + 8] for t in range(n // 8)]
    rows = lax.broadcasted_iota(jnp.int32, (8, 2 * n), 0)
    full = lambda v: jnp.broadcast_to(v, (8, 2 * n))
    for k in range(0, n, 4):
        at, r0 = k // 8, k % 8
        c = [[full(v[:, k + j : k + j + 1]) for j in range(4)] for v in w]
        lines = [full(w[at][r0 + i : r0 + i + 1]) for i in range(4)]
        p = block_inverse({(i, j): c[at][j][r0 + i : r0 + i + 1] for i in range(4) for j in range(i, 4)})
        t = [(p[i][0] * lines[0] + p[i][1] * lines[1]) + (p[i][2] * lines[2] + p[i][3] * lines[3]) for i in range(4)]
        for g in range(n // 8):
            w[g] = w[g] - ((c[g][0] * t[0] + c[g][1] * t[1]) + (c[g][2] * t[2] + c[g][3] * t[3]))
        for i in range(4):
            w[at] = jnp.where(rows == r0 + i, t[i], w[at])
    return jnp.concatenate(w, axis=0)[:, n:]


def spread(lv, av, lt, lw, gp):
    lhi, llo = split(lv)
    hi32, lo32 = lhi.astype(F32), llo.astype(F32)
    ones = jnp.ones((3, ROWS), F32)
    k_rows = [hi32, hi32, lo32] + split_rows(av) + [ones, jnp.zeros((58, ROWS), F32)]
    lt[...] = jnp.concatenate(k_rows, axis=0).T.astype(BF)
    lw[0:64] = lhi
    lw[64:128] = llo
    lw[128:144] = jnp.ones((16, ROWS), BF)
    last = ((1,), (1,))
    both = jnp.concatenate([lhi, llo], axis=0)
    g = dot(both, lhi, last)
    g = g[0:64] + g[64:128] + dot(lhi, llo, last)
    gp[0:32] = jnp.concatenate([g[0:32], g[32:64]], axis=1)
    l1 = dot(jnp.ones((16, ROWS), BF), both, last)[0:1]
    gp[32:33] = jnp.concatenate([l1[:, 0:64] + l1[:, 64:128], jnp.zeros((1, 64), F32)], axis=1)


SPREAD = [((ROWS, 256), BF), ((144, ROWS), BF), ((40, 128), F32)]


def prep_kernel(panel, b, l, a, ts, panel_out, b_out, l_out, a_out, tsb, lt, lw, gp, ts_in, sems):
    pairs = ((panel, panel_out), (b, b_out), (l, l_out), (a, a_out), (ts, ts_in))
    moves = [pltpu.make_async_copy(src, dst, sems.at[i]) for i, (src, dst) in enumerate(pairs)]
    for move in moves:
        move.start()
    for move in moves[1:]:
        move.wait()
    tsb[...] = jnp.broadcast_to(ts_in[...].astype(F32), (128, ROWS)).T
    spread(l_out[...], a_out[...], lt, lw, gp)
    moves[0].wait()


def prep(*operands):
    outs = [((ROWS, DAYS), F32), ((1, DAYS), F32), ((RANK, ROWS), F32), ((1, ROWS), F32), ((ROWS, 128), F32)] + SPREAD
    return pl.pallas_call(
        prep_kernel,
        in_specs=[pl.BlockSpec(memory_space=pltpu.HBM)] * 5,
        out_specs=[vmem()] * len(outs),
        out_shape=[pltpu.VMEM(shape, dtype) for shape, dtype in outs],
        scratch_shapes=[pltpu.VMEM((1, ROWS), jnp.int32), pltpu.SemaphoreType.DMA((5,))],
        compiler_params=pltpu.CompilerParams(vmem_limit_bytes=16 << 20),
        name="prep",
    )(*[pltpu.with_memory_space_constraint(x, pltpu.HBM) for x in operands])


def first_kernel(k_ref, panel, f, b, a, tsb, lt, lw, gp, *rest, own):
    if own:
        l, acc_in, out, dhi, dlo, rm = rest
    else:
        out, dhi, dlo, acc_out = rest
    k = k_ref[0]
    half = k if own else 1 - k
    start = pl.multiple_of(half * HALF, HALF)
    lane = lax.broadcasted_iota(jnp.int32, (ROWS, 128), 1)
    left = tsb[...] - (lane + start).astype(F32)
    run = acc_in[...] if own else jnp.zeros((ROWS, 128), F32)
    a_sum = jnp.broadcast_to(jnp.sum(a[...], axis=1, keepdims=True), (1, 128))

    def fit(j):
        fhi, flo = split(f[:, BLK * j : BLK * (j + 1)])
        bv = b[:, pl.ds(start + BLK * j, BLK)]
        aux = jnp.concatenate([jnp.ones((3, BLK), F32)] + split_rows(bv) + [jnp.zeros((58, BLK), F32)], axis=0)
        return dot(lt[...], jnp.concatenate([fhi, flo, fhi, aux.astype(BF)], axis=0))

    def weigh(j):
        whole = slice(BLK * j, BLK * (j + 1))
        r1 = dot(lw[...], dhi[:, whole])
        r2 = dot(lw[...], dlo[:, whole])
        w = r1[0:64] + r1[64:128] + r2[0:64]
        day_sum = r1[128:129] + r2[128:129]
        extra = [day_sum[:, 128 * q : 128 * (q + 1)] for q in range(4)]
        line = gp[32:33, :]
        if own and j == NBLK - 1:
            means = dot_exact(jnp.ones((8, 128), F32), run, ((1,), (1,))) * (1.0 / DAYS)
            rm[...] = means[0:1]
            lr = dot_exact(means, l[...], ((1,), (1,)))[0:1]
            line = jnp.concatenate([line[:, 0:64], lr], axis=1)
        extra += [gp[8 * j : 8 * j + 8], line, a_sum, jnp.zeros((2, 128), F32)]
        extra = jnp.concatenate(extra, axis=0)
        for i in range(8):
            for t in range(2):
                at = BROWS * j + CHUNK * (2 * i + t)
                out[at : at + 8, :] = w[8 * i : 8 * i + 8, 256 * t : 256 * t + 128]
                out[at + 8 : at + 16, :] = w[8 * i : 8 * i + 8, 256 * t + 128 : 256 * t + 256]
                out[at + 16 : at + 17, :] = extra[2 * i + t : 2 * i + t + 1]

    s = fit(0)
    for j in range(NBLK):
        following = fit(j + 1) if j + 1 < NBLK else None
        for q in range(BLK // 128):
            at = BLK * j + 128 * q
            cols = slice(at, at + 128)
            x = panel[:, pl.ds(start + at, 128)]
            d = jnp.where(left > float(at), x - s[:, 128 * q : 128 * (q + 1)], 0.0)
            hi, lo = split(d)
            dhi[:, cols] = hi
            dlo[:, cols] = lo
            run = run + d
        s = following
        if j:
            weigh(j - 1)
    weigh(NBLK - 1)
    if not own:
        acc_out[...] = run


def vmem():
    return pl.BlockSpec(memory_space=pltpu.VMEM)


def smem():
    return pl.BlockSpec(memory_space=pltpu.SMEM)


def call(kernel, name, scalars, operands, outs, scratch=(), place=pltpu.VMEM):
    return pl.pallas_call(
        kernel,
        in_specs=[smem()] * len(scalars) + [vmem()] * len(operands),
        out_specs=[vmem()] * len(outs),
        out_shape=[place(shape, dtype) for shape, dtype in outs],
        scratch_shapes=list(scratch),
        compiler_params=pltpu.CompilerParams(vmem_limit_bytes=16 << 20),
        name=name,
    )(*scalars, *[pltpu.with_memory_space_constraint(x, pltpu.VMEM) for x in operands])


def first_other(k, panel, f, b, a, *spreads):
    outs = [((PAY, 128), F32), ((ROWS, HALF), BF), ((ROWS, HALF), BF), ((ROWS, 128), F32)]
    return call(functools.partial(first_kernel, own=False), "first_other", [k], [panel, f, b, a, *spreads], outs)


def first_own(k, panel, f, b, a, *rest):
    outs = [((PAY, 128), F32), ((ROWS, HALF), BF), ((ROWS, HALF), BF), ((1, ROWS), F32)]
    return call(functools.partial(first_kernel, own=True), "first_own", [k], [panel, f, b, a, *rest], outs)


def sum_kernel(x, out):
    slab = x[0 : 8 * CHUNK, :]
    for g in range(1, 8):
        slab = slab + x[8 * CHUNK * g : 8 * CHUNK * (g + 1), :]
    total = slab[0:CHUNK]
    for c in range(1, 8):
        total = total + slab[CHUNK * c : CHUNK * (c + 1)]
    slab = jnp.concatenate([total] * 8, axis=0)
    for g in range(8):
        out[8 * CHUNK * g : 8 * CHUNK * (g + 1), :] = slab


def sum_and_copy(x):
    return call(sum_kernel, "sum_and_copy", [], [x], [((PAY, 128), F32)])[0]


def extra_row(x, j, e):
    at = BROWS * j + CHUNK * e + 16
    return x[at : at + 1, :]


def gram_kernel(x, out):
    packed = jnp.concatenate([extra_row(x, j, 4 + e) for j in range(4) for e in range(8)], axis=0)
    g = jnp.concatenate([packed[:, 0:64], packed[:, 64:128]], axis=0)
    row = lax.broadcasted_iota(jnp.int32, (RANK, RANK), 0)
    col = lax.broadcasted_iota(jnp.int32, (RANK, RANK), 1)
    out[...] = inverse(g + jnp.where(row == col, RIDGE, 0.0))


def gram_inverse(x):
    return call(gram_kernel, "gram_inverse", [], [x], [((RANK, RANK), F32)])[0]


def second_kernel(k_ref, own, oth, ginv, f_own, f_oth, b_ref, dhi_own, dlo_own, dhi_oth, dlo_oth, l, a, rm, *rest, final):
    if final:
        bn, ln, an, shard, fn_own, fn_oth, bt, new_rows, turn = rest
    else:
        bn, ln, an, fn_own, fn_oth, lt, lw, gp, bt, new_rows = rest
    k = k_ref[0]
    starts = [pl.multiple_of(k * HALF, HALF), pl.multiple_of((1 - k) * HALF, HALF)]
    sums = [jnp.concatenate([extra_row(x, j, q) for j in range(4) for q in range(4)], axis=1) for x in (own, oth)]
    mean_d = jnp.sum(sums[0] + sums[1], axis=1, keepdims=True) * (1.0 / (UNITS * DAYS))
    mean_b = jnp.sum(b_ref[...], axis=1, keepdims=True) * (1.0 / DAYS)
    mean_a = extra_row(own, 3, 13)[:, 0:1] * (1.0 / UNITS)
    lane = lax.broadcasted_iota(jnp.int32, (1, 128), 1)
    l_own, l_oth = extra_row(own, 3, 12), extra_row(oth, 3, 12)
    lines = l_own + jnp.where(lane >= 64, l_oth, 0.0)
    turned = jnp.broadcast_to(lines, (128, 128)).T
    l1 = turned[0:64, 0:1]
    u = (mean_d + mean_a) * l1 - turned[64:128, 0:1]
    ghi, glo = split(ginv[...])
    gcat = jnp.concatenate([ghi, ghi, glo], axis=1)
    f1 = jnp.zeros((RANK, 128), F32)
    fb = jnp.zeros((RANK, 128), F32)
    for side, (x, f, fn, col, start) in enumerate(
        ((own, f_own, fn_own, sums[0], starts[0]), (oth, f_oth, fn_oth, sums[1], starts[1]))
    ):
        v = mean_d + mean_b - col * (1.0 / UNITS)
        bn[:, pl.ds(start, HALF)] = b_ref[:, pl.ds(start, HALF)] - v
        def solved(j, x=x, f=f, v=v):
            cols = slice(BLK * j, BLK * (j + 1))
            lines = []
            for i in range(8):
                tiles = []
                for t in range(2):
                    at = BROWS * j + CHUNK * (2 * i + t)
                    tiles += [x[at : at + 8, :], x[at + 8 : at + 16, :]]
                lines.append(jnp.concatenate(tiles, axis=1))
            fv = f[:, cols]
            r = jnp.concatenate(lines, axis=0) + u + l1 * v[:, cols] - fv
            rhi, rlo = split(r)
            return fv, dot(gcat, jnp.concatenate([rhi, rlo, rhi], axis=0))

        pending = solved(0)
        for j in range(NBLK):
            cols = slice(BLK * j, BLK * (j + 1))
            fv, step = pending
            if j + 1 < NBLK:
                pending = solved(j + 1)
            new = fv + step
            fn[:, cols] = new
            nhi, nlo = split(new)
            ohi, olo = split(fv)
            both = jnp.concatenate([nhi, nlo, ohi, olo], axis=0).T
            at = HALF * side + BLK * j
            bt[at : at + BLK, :] = both
            new_rows[:, at : at + BLK] = jnp.concatenate([nhi, nlo], axis=0)
            nb = new * v[:, cols]
            for q in range(BLK // 128):
                f1 = f1 + new[:, 128 * q : 128 * (q + 1)]
                fb = fb + nb[:, 128 * q : 128 * (q + 1)]
    hx = dot(new_rows[...], bt[...])
    f1 = jnp.sum(f1, axis=1, keepdims=True)
    fb = jnp.sum(fb, axis=1, keepdims=True)
    da = mean_d + mean_a - rm[...]
    a_new = a[...] - da
    an[...] = a_new
    row = lax.broadcasted_iota(jnp.int32, (RANK, RANK), 0)
    col = lax.broadcasted_iota(jnp.int32, (RANK, RANK), 1)
    h = hx[0:64, 0:64] + hx[0:64, 64:128] + hx[64:128, 0:64]
    xn = hx[0:64, 128:192] + hx[0:64, 192:256] + hx[64:128, 128:192]
    z = jnp.zeros((RANK, ROWS), F32)
    for at, hi, lo in ((0, dhi_own, dlo_own), (HALF, dhi_oth, dlo_oth)):
        days = slice(at, at + HALF)
        part = dot(new_rows[:, days], hi[...], ((1,), (1,)))
        z = z + part[0:64] + part[64:128] + dot(new_rows[0:64, days], lo[...], ((1,), (1,)))
    hinv = inverse(h + jnp.where(row == col, RIDGE, 0.0))
    p = dot_exact(xn, l[...]) + f1 * da + fb + z
    l_new = dot_exact(hinv, p)
    ln[...] = l_new
    if final:
        tile = pl.multiple_of(128 * k_ref[2], 128)
        mine = jnp.where(k_ref[1] == 1, fn_own[:, pl.ds(tile, 128)], fn_oth[:, pl.ds(tile, 128)])
        turn[...] = mine.T
        shard[...] = turn[pl.ds(pl.multiple_of(32 * k_ref[3], 32), 32), :]
    else:
        spread(l_new, a_new, lt, lw, gp)


def second(k, final, *operands):
    outs = [((1, DAYS), F32), ((RANK, ROWS), F32), ((1, ROWS), F32)]
    kernel = functools.partial(second_kernel, final=final)
    half = ((RANK, HALF), F32)
    work = [pltpu.VMEM((DAYS, 256), BF), pltpu.VMEM((128, DAYS), BF)]
    if final:
        scratch = [pltpu.VMEM(*half), pltpu.VMEM(*half), *work, pltpu.VMEM((128, RANK), F32)]
        outs = outs + [((32, RANK), F32)]
        return call(kernel, "second_last", [k], operands, outs, scratch, jax.ShapeDtypeStruct)
    return call(kernel, "second", [k], operands, outs + [half, half] + SPREAD, work)


def pack_kernel(k_ref, x, out):
    v = x[...].T
    packed = jnp.concatenate([v[16 * q : 16 * q + 16] for q in range(4)], axis=1)
    packed = pltpu.roll(packed, 32 * k_ref[3], 1)
    for c in range(PEERS):
        out[16 * c : 16 * c + 16, :] = packed


def unpack_kernel(k_ref, own, oth, f_own, f_oth):
    k = k_ref[0]
    even = k == 0
    slot = lax.broadcasted_iota(jnp.int32, (16, 128), 1) // 32
    for j in range(16):
        for dst, half in ((f_own, k), (f_oth, 1 - k)):
            parts = []
            for m in range(4):
                at = pl.multiple_of((half * 32 + 2 * j + m // 2) * 16, 16)
                x, y = own[pl.ds(at, 16), :], oth[pl.ds(at, 16), :]
                parts.append(jnp.where(even, x, y) if m % 2 == 0 else jnp.where(even, y, x))
            for q in range(4):
                total = parts[-q % 4]
                for t in range(1, 4):
                    total = jnp.where(slot == t, parts[(t - q) % 4], total)
                if q:
                    total = pltpu.roll(total, 128 - 32 * q, 1)
                dst[16 * q : 16 * q + 16, 128 * j : 128 * j + 128] = total


def gather_factors(k, f):
    lines = call(pack_kernel, "pack_factors", [k], [f.T], [((PEERS * 16, 128), F32)])[0]
    own = swap_chips(lines)
    oth = other_core(own)
    return call(unpack_kernel, "unpack_factors", [k], [own, oth], [((RANK, HALF), F32)] * 2)


def swap_chips(lines):
    shape = lines.shape
    parts = lines.reshape(PEERS, 1, -1)
    return lax.all_to_all(parts, CHIPS, 0, 0, tiled=True).reshape(shape)


def other_core(x):
    return lax.ppermute(x, CORE, [(0, 1), (1, 0)])


def body(panel, treat_start, loading_init, factor_init, unit_init, day_init):
    core = lax.axis_index(CORE)
    device = 2 * lax.axis_index(CHIPS) + core
    in_own = (device >> 6) == core
    k = jnp.stack([core, in_own.astype(jnp.int32), (device & 63) >> 2, device & 3]).astype(jnp.int32)
    f_own, f_oth = gather_factors(k, factor_init)
    ts = treat_start.reshape(1, ROWS)
    panel, b, loading, a, tsb, *spreads = prep(
        panel, day_init.reshape(1, DAYS), loading_init, unit_init.reshape(1, ROWS), ts
    )
    for sweep in range(SWEEPS):
        sent, dhi_oth, dlo_oth, acc = first_other(k, panel, f_oth, b, a, tsb, *spreads)
        arrived = other_core(sent)
        kept, dhi_own, dlo_own, rm = first_own(k, panel, f_own, b, a, tsb, *spreads, loading, acc)
        summed = sum_and_copy(swap_chips(kept + arrived))
        own = swap_chips(summed)
        oth = other_core(own)
        ginv = gram_inverse(own)
        final = sweep == SWEEPS - 1
        b, loading, a, *rest = second(
            k, final, own, oth, ginv, f_own, f_oth, b, dhi_own, dlo_own, dhi_oth, dlo_oth, loading, a, rm
        )
        if not final:
            f_own, f_oth, *spreads = rest
    return (loading, rest[0].T, a.reshape(ROWS), b.reshape(DAYS))


def solution(mesh):
    finer = Mesh(
        mesh.devices.reshape(mesh.shape["gx"], mesh.shape["gy"], 4, 2), ("gx", "gy", "gz_0", "gz_1")
    )
    return jax.shard_map(
        body,
        mesh=finer,
        in_specs=(
            P(GX_GY_GZ, None),
            P(GX_GY_GZ),
            P(None, GX_GY_GZ),
            P(None, GX_GY_GZ),
            P(GX_GY_GZ),
            P(),
        ),
        out_specs=(P(None, GX_GY_GZ), P(None, GX_GY_GZ), P(GX_GY_GZ), P()),
        check_vma=False,
    )
```

```python
import functools

import jax
import jax.numpy as jnp
from jax import lax
from jax.experimental import pallas as pl
from jax.experimental.pallas import tpu as pltpu
from jax.sharding import Mesh
from jax.sharding import PartitionSpec as P

SWEEPS = 2
RIDGE = 1.0
GX_GY_GZ = ("gx", "gy", "gz_0", "gz_1")
CHIPS = ("gx", "gy", "gz_0")
CORE = "gz_1"

RANK = 64
ROWS = 256
DAYS = 4096
HALF = 2048
UNITS = 32768
BLK = 512
NBLK = HALF // BLK
PEERS = 64
CHUNK = 17
BROWS = 16 * CHUNK
PAY = PEERS * CHUNK
F32 = jnp.float32
BF = jnp.bfloat16


def dot(x, y, dims=((1,), (0,))):
    return lax.dot_general(x, y, (dims, ((), ())), preferred_element_type=F32)


def dot_exact(x, y, dims=((1,), (0,))):
    return lax.dot_general(x, y, (dims, ((), ())), preferred_element_type=F32, precision=lax.Precision.HIGHEST)


def split(x):
    hi = x.astype(BF)
    return hi, (x - hi.astype(F32)).astype(BF)


def split_rows(x):
    hi = x.astype(BF).astype(F32)
    mid = (x - hi).astype(BF).astype(F32)
    return [hi, mid, x - hi - mid]


def pair_inverse(a, b, d):
    q = 1.0 / (a * d - b * b)
    return d * q, -b * q, a * q


def block_inverse(p):
    a0, a1, a2 = pair_inverse(p[0, 0], p[0, 1], p[1, 1])
    top, low = (a0, a1), (a1, a2)
    ab = [[r[0] * p[0, c] + r[1] * p[1, c] for c in (2, 3)] for r in (top, low)]
    s00 = p[2, 2] - (p[0, 2] * ab[0][0] + p[1, 2] * ab[1][0])
    s01 = p[2, 3] - (p[0, 2] * ab[0][1] + p[1, 2] * ab[1][1])
    s11 = p[3, 3] - (p[0, 3] * ab[0][1] + p[1, 3] * ab[1][1])
    s0, s1, s2 = pair_inverse(s00, s01, s11)
    k = [[-(r[0] * s0 + r[1] * s1), -(r[0] * s1 + r[1] * s2)] for r in ab]
    c00 = a0 - (k[0][0] * ab[0][0] + k[0][1] * ab[0][1])
    c01 = a1 - (k[0][0] * ab[1][0] + k[0][1] * ab[1][1])
    c11 = a2 - (k[1][0] * ab[1][0] + k[1][1] * ab[1][1])
    return [
        [c00, c01, k[0][0], k[0][1]],
        [c01, c11, k[1][0], k[1][1]],
        [k[0][0], k[1][0], s0, s1],
        [k[0][1], k[1][1], s1, s2],
    ]


def inverse(m):
    n = m.shape[0]
    row = lax.broadcasted_iota(jnp.int32, (n, n), 0)
    col = lax.broadcasted_iota(jnp.int32, (n, n), 1)
    w = jnp.concatenate([m, (row == col).astype(F32)], axis=1)
    w = [w[8 * t : 8 * t + 8] for t in range(n // 8)]
    rows = lax.broadcasted_iota(jnp.int32, (8, 2 * n), 0)
    full = lambda v: jnp.broadcast_to(v, (8, 2 * n))
    for k in range(0, n, 4):
        at, r0 = k // 8, k % 8
        c = [[full(v[:, k + j : k + j + 1]) for j in range(4)] for v in w]
        lines = [full(w[at][r0 + i : r0 + i + 1]) for i in range(4)]
        p = block_inverse({(i, j): c[at][j][r0 + i : r0 + i + 1] for i in range(4) for j in range(i, 4)})
        t = [(p[i][0] * lines[0] + p[i][1] * lines[1]) + (p[i][2] * lines[2] + p[i][3] * lines[3]) for i in range(4)]
        for g in range(n // 8):
            w[g] = w[g] - ((c[g][0] * t[0] + c[g][1] * t[1]) + (c[g][2] * t[2] + c[g][3] * t[3]))
        for i in range(4):
            w[at] = jnp.where(rows == r0 + i, t[i], w[at])
    return jnp.concatenate(w, axis=0)[:, n:]


def spread(lv, av, lt, lw, gp):
    lhi, llo = split(lv)
    hi32, lo32 = lhi.astype(F32), llo.astype(F32)
    ones = jnp.ones((3, ROWS), F32)
    k_rows = [hi32, hi32, lo32] + split_rows(av) + [ones, jnp.zeros((58, ROWS), F32)]
    lt[...] = jnp.concatenate(k_rows, axis=0).T.astype(BF)
    lw[0:64] = lhi
    lw[64:128] = llo
    lw[128:144] = jnp.ones((16, ROWS), BF)
    last = ((1,), (1,))
    both = jnp.concatenate([lhi, llo], axis=0)
    g = dot(both, lhi, last)
    g = g[0:64] + g[64:128] + dot(lhi, llo, last)
    gp[0:32] = jnp.concatenate([g[0:32], g[32:64]], axis=1)
    l1 = dot(jnp.ones((16, ROWS), BF), both, last)[0:1]
    gp[32:33] = jnp.concatenate([l1[:, 0:64] + l1[:, 64:128], jnp.zeros((1, 64), F32)], axis=1)


SPREAD = [((ROWS, 256), BF), ((144, ROWS), BF), ((40, 128), F32)]


def prep_kernel(panel, b, l, a, ts, panel_out, b_out, l_out, a_out, tsb, lt, lw, gp, ts_in, sems):
    pairs = ((panel, panel_out), (b, b_out), (l, l_out), (a, a_out), (ts, ts_in))
    moves = [pltpu.make_async_copy(src, dst, sems.at[i]) for i, (src, dst) in enumerate(pairs)]
    for move in moves:
        move.start()
    for move in moves[1:]:
        move.wait()
    tsb[...] = jnp.broadcast_to(ts_in[...].astype(F32), (128, ROWS)).T
    spread(l_out[...], a_out[...], lt, lw, gp)
    moves[0].wait()


def prep(*operands):
    outs = [((ROWS, DAYS), F32), ((1, DAYS), F32), ((RANK, ROWS), F32), ((1, ROWS), F32), ((ROWS, 128), F32)] + SPREAD
    return pl.pallas_call(
        prep_kernel,
        in_specs=[pl.BlockSpec(memory_space=pltpu.HBM)] * 5,
        out_specs=[vmem()] * len(outs),
        out_shape=[pltpu.VMEM(shape, dtype) for shape, dtype in outs],
        scratch_shapes=[pltpu.VMEM((1, ROWS), jnp.int32), pltpu.SemaphoreType.DMA((5,))],
        compiler_params=pltpu.CompilerParams(vmem_limit_bytes=16 << 20),
        name="prep",
    )(*[pltpu.with_memory_space_constraint(x, pltpu.HBM) for x in operands])


def first_kernel(panel, f, b, a, tsb, lt, lw, gp, *rest, own):
    if own:
        l, acc_in, out, dhi, dlo, rm = rest
    else:
        out, dhi, dlo, acc_out = rest
    k = lax.axis_index(CORE)
    half = k if own else 1 - k
    start = pl.multiple_of(half * HALF, HALF)
    lane = lax.broadcasted_iota(jnp.int32, (ROWS, 128), 1)
    left = tsb[...] - (lane + start).astype(F32)
    run = acc_in[...] if own else jnp.zeros((ROWS, 128), F32)
    a_sum = jnp.broadcast_to(jnp.sum(a[...], axis=1, keepdims=True), (1, 128))

    def fit(j):
        fhi, flo = split(f[:, BLK * j : BLK * (j + 1)])
        bv = b[:, pl.ds(start + BLK * j, BLK)]
        aux = jnp.concatenate([jnp.ones((3, BLK), F32)] + split_rows(bv) + [jnp.zeros((58, BLK), F32)], axis=0)
        return dot(lt[...], jnp.concatenate([fhi, flo, fhi, aux.astype(BF)], axis=0))

    def weigh(j):
        whole = slice(BLK * j, BLK * (j + 1))
        r1 = dot(lw[...], dhi[:, whole])
        r2 = dot(lw[...], dlo[:, whole])
        w = r1[0:64] + r1[64:128] + r2[0:64]
        day_sum = r1[128:129] + r2[128:129]
        extra = [day_sum[:, 128 * q : 128 * (q + 1)] for q in range(4)]
        line = gp[32:33, :]
        if own and j == NBLK - 1:
            means = dot_exact(jnp.ones((8, 128), F32), run, ((1,), (1,))) * (1.0 / DAYS)
            rm[...] = means[0:1]
            lr = dot_exact(means, l[...], ((1,), (1,)))[0:1]
            line = jnp.concatenate([line[:, 0:64], lr], axis=1)
        extra += [gp[8 * j : 8 * j + 8], line, a_sum, jnp.zeros((2, 128), F32)]
        extra = jnp.concatenate(extra, axis=0)
        for i in range(8):
            for t in range(2):
                at = BROWS * j + CHUNK * (2 * i + t)
                out[at : at + 8, :] = w[8 * i : 8 * i + 8, 256 * t : 256 * t + 128]
                out[at + 8 : at + 16, :] = w[8 * i : 8 * i + 8, 256 * t + 128 : 256 * t + 256]
                out[at + 16 : at + 17, :] = extra[2 * i + t : 2 * i + t + 1]

    s = fit(0)
    for j in range(NBLK):
        following = fit(j + 1) if j + 1 < NBLK else None
        for q in range(BLK // 128):
            at = BLK * j + 128 * q
            cols = slice(at, at + 128)
            x = panel[:, pl.ds(start + at, 128)]
            d = jnp.where(left > float(at), x - s[:, 128 * q : 128 * (q + 1)], 0.0)
            hi, lo = split(d)
            dhi[:, cols] = hi
            dlo[:, cols] = lo
            run = run + d
        s = following
        if j:
            weigh(j - 1)
    weigh(NBLK - 1)
    if not own:
        acc_out[...] = run


def vmem():
    return pl.BlockSpec(memory_space=pltpu.VMEM)


def device_index():
    gx, gy, gz_0, gz_1 = [lax.axis_index(axis) for axis in GX_GY_GZ]
    return ((gx * 4 + gy) * 4 + gz_0) * 2 + gz_1


def call(kernel, name, operands, outs, scratch=(), place=pltpu.VMEM):
    return pl.pallas_call(
        kernel,
        in_specs=[vmem()] * len(operands),
        out_specs=[vmem()] * len(outs),
        out_shape=[place(shape, dtype) for shape, dtype in outs],
        scratch_shapes=list(scratch),
        compiler_params=pltpu.CompilerParams(vmem_limit_bytes=16 << 20),
        name=name,
    )(*[pltpu.with_memory_space_constraint(x, pltpu.VMEM) for x in operands])


def first_other(panel, f, b, a, *spreads):
    outs = [((PAY, 128), F32), ((ROWS, HALF), BF), ((ROWS, HALF), BF), ((ROWS, 128), F32)]
    return call(functools.partial(first_kernel, own=False), "first_other", [panel, f, b, a, *spreads], outs)


def first_own(panel, f, b, a, *rest):
    outs = [((PAY, 128), F32), ((ROWS, HALF), BF), ((ROWS, HALF), BF), ((1, ROWS), F32)]
    return call(functools.partial(first_kernel, own=True), "first_own", [panel, f, b, a, *rest], outs)


def sum_kernel(x, out):
    slab = x[0 : 8 * CHUNK, :]
    for g in range(1, 8):
        slab = slab + x[8 * CHUNK * g : 8 * CHUNK * (g + 1), :]
    total = slab[0:CHUNK]
    for c in range(1, 8):
        total = total + slab[CHUNK * c : CHUNK * (c + 1)]
    slab = jnp.concatenate([total] * 8, axis=0)
    for g in range(8):
        out[8 * CHUNK * g : 8 * CHUNK * (g + 1), :] = slab


def sum_and_copy(x):
    return call(sum_kernel, "sum_and_copy", [x], [((PAY, 128), F32)])[0]


def extra_row(x, j, e):
    at = BROWS * j + CHUNK * e + 16
    return x[at : at + 1, :]


def gram_kernel(x, out):
    packed = jnp.concatenate([extra_row(x, j, 4 + e) for j in range(4) for e in range(8)], axis=0)
    g = jnp.concatenate([packed[:, 0:64], packed[:, 64:128]], axis=0)
    row = lax.broadcasted_iota(jnp.int32, (RANK, RANK), 0)
    col = lax.broadcasted_iota(jnp.int32, (RANK, RANK), 1)
    out[...] = inverse(g + jnp.where(row == col, RIDGE, 0.0))


def gram_inverse(x):
    return call(gram_kernel, "gram_inverse", [x], [((RANK, RANK), F32)])[0]


def second_kernel(own, oth, ginv, f_own, f_oth, b_ref, dhi_own, dlo_own, dhi_oth, dlo_oth, l, a, rm, *rest, final):
    if final:
        bn, ln, an, shard, fn_own, fn_oth, bt, new_rows, turn = rest
    else:
        bn, ln, an, fn_own, fn_oth, lt, lw, gp, bt, new_rows = rest
    k = lax.axis_index(CORE)
    starts = [pl.multiple_of(k * HALF, HALF), pl.multiple_of((1 - k) * HALF, HALF)]
    sums = [jnp.concatenate([extra_row(x, j, q) for j in range(4) for q in range(4)], axis=1) for x in (own, oth)]
    mean_d = jnp.sum(sums[0] + sums[1], axis=1, keepdims=True) * (1.0 / (UNITS * DAYS))
    mean_b = jnp.sum(b_ref[...], axis=1, keepdims=True) * (1.0 / DAYS)
    mean_a = extra_row(own, 3, 13)[:, 0:1] * (1.0 / UNITS)
    lane = lax.broadcasted_iota(jnp.int32, (1, 128), 1)
    l_own, l_oth = extra_row(own, 3, 12), extra_row(oth, 3, 12)
    lines = l_own + jnp.where(lane >= 64, l_oth, 0.0)
    turned = jnp.broadcast_to(lines, (128, 128)).T
    l1 = turned[0:64, 0:1]
    u = (mean_d + mean_a) * l1 - turned[64:128, 0:1]
    ghi, glo = split(ginv[...])
    gcat = jnp.concatenate([ghi, ghi, glo], axis=1)
    f1 = jnp.zeros((RANK, 128), F32)
    fb = jnp.zeros((RANK, 128), F32)
    for side, (x, f, fn, col, start) in enumerate(
        ((own, f_own, fn_own, sums[0], starts[0]), (oth, f_oth, fn_oth, sums[1], starts[1]))
    ):
        v = mean_d + mean_b - col * (1.0 / UNITS)
        bn[:, pl.ds(start, HALF)] = b_ref[:, pl.ds(start, HALF)] - v
        def solved(j, x=x, f=f, v=v):
            cols = slice(BLK * j, BLK * (j + 1))
            lines = []
            for i in range(8):
                tiles = []
                for t in range(2):
                    at = BROWS * j + CHUNK * (2 * i + t)
                    tiles += [x[at : at + 8, :], x[at + 8 : at + 16, :]]
                lines.append(jnp.concatenate(tiles, axis=1))
            fv = f[:, cols]
            r = jnp.concatenate(lines, axis=0) + u + l1 * v[:, cols] - fv
            rhi, rlo = split(r)
            return fv, dot(gcat, jnp.concatenate([rhi, rlo, rhi], axis=0))

        pending = solved(0)
        for j in range(NBLK):
            cols = slice(BLK * j, BLK * (j + 1))
            fv, step = pending
            if j + 1 < NBLK:
                pending = solved(j + 1)
            new = fv + step
            fn[:, cols] = new
            nhi, nlo = split(new)
            ohi, olo = split(fv)
            both = jnp.concatenate([nhi, nlo, ohi, olo], axis=0).T
            at = HALF * side + BLK * j
            bt[at : at + BLK, :] = both
            new_rows[:, at : at + BLK] = jnp.concatenate([nhi, nlo], axis=0)
            nb = new * v[:, cols]
            for q in range(BLK // 128):
                f1 = f1 + new[:, 128 * q : 128 * (q + 1)]
                fb = fb + nb[:, 128 * q : 128 * (q + 1)]
    hx = dot(new_rows[...], bt[...])
    f1 = jnp.sum(f1, axis=1, keepdims=True)
    fb = jnp.sum(fb, axis=1, keepdims=True)
    da = mean_d + mean_a - rm[...]
    a_new = a[...] - da
    an[...] = a_new
    row = lax.broadcasted_iota(jnp.int32, (RANK, RANK), 0)
    col = lax.broadcasted_iota(jnp.int32, (RANK, RANK), 1)
    h = hx[0:64, 0:64] + hx[0:64, 64:128] + hx[64:128, 0:64]
    xn = hx[0:64, 128:192] + hx[0:64, 192:256] + hx[64:128, 128:192]
    z = jnp.zeros((RANK, ROWS), F32)
    for at, hi, lo in ((0, dhi_own, dlo_own), (HALF, dhi_oth, dlo_oth)):
        days = slice(at, at + HALF)
        part = dot(new_rows[:, days], hi[...], ((1,), (1,)))
        z = z + part[0:64] + part[64:128] + dot(new_rows[0:64, days], lo[...], ((1,), (1,)))
    hinv = inverse(h + jnp.where(row == col, RIDGE, 0.0))
    p = dot_exact(xn, l[...]) + f1 * da + fb + z
    l_new = dot_exact(hinv, p)
    ln[...] = l_new
    if final:
        device = device_index()
        tile = pl.multiple_of(128 * ((device & 63) // 4), 128)
        mine = jnp.where(device // 64 == k, fn_own[:, pl.ds(tile, 128)], fn_oth[:, pl.ds(tile, 128)])
        turn[...] = mine.T
        shard[...] = turn[pl.ds(pl.multiple_of(32 * (device & 3), 32), 32), :]
    else:
        spread(l_new, a_new, lt, lw, gp)


def second(final, *operands):
    outs = [((1, DAYS), F32), ((RANK, ROWS), F32), ((1, ROWS), F32)]
    kernel = functools.partial(second_kernel, final=final)
    half = ((RANK, HALF), F32)
    work = [pltpu.VMEM((DAYS, 256), BF), pltpu.VMEM((128, DAYS), BF)]
    if final:
        scratch = [pltpu.VMEM(*half), pltpu.VMEM(*half), *work, pltpu.VMEM((128, RANK), F32)]
        outs = outs + [((32, RANK), F32)]
        return call(kernel, "second_last", operands, outs, scratch, jax.ShapeDtypeStruct)
    return call(kernel, "second", operands, outs + [half, half] + SPREAD, work)


def pack_kernel(x, out):
    v = x[...].T
    packed = jnp.concatenate([v[16 * q : 16 * q + 16] for q in range(4)], axis=1)
    packed = pltpu.roll(packed, 32 * (device_index() & 3), 1)
    for c in range(PEERS):
        out[16 * c : 16 * c + 16, :] = packed


def unpack_kernel(own, oth, f_own, f_oth):
    k = lax.axis_index(CORE)
    even = k == 0
    slot = lax.broadcasted_iota(jnp.int32, (16, 128), 1) // 32
    for j in range(16):
        for dst, half in ((f_own, k), (f_oth, 1 - k)):
            parts = []
            for m in range(4):
                at = pl.multiple_of((half * 32 + 2 * j + m // 2) * 16, 16)
                x, y = own[pl.ds(at, 16), :], oth[pl.ds(at, 16), :]
                parts.append(jnp.where(even, x, y) if m % 2 == 0 else jnp.where(even, y, x))
            for q in range(4):
                total = parts[-q % 4]
                for t in range(1, 4):
                    total = jnp.where(slot == t, parts[(t - q) % 4], total)
                if q:
                    total = pltpu.roll(total, 128 - 32 * q, 1)
                dst[16 * q : 16 * q + 16, 128 * j : 128 * j + 128] = total


def gather_factors(f):
    lines = call(pack_kernel, "pack_factors", [f.T], [((PEERS * 16, 128), F32)])[0]
    own = swap_chips(lines)
    oth = other_core(own)
    return call(unpack_kernel, "unpack_factors", [own, oth], [((RANK, HALF), F32)] * 2)


def swap_chips(lines):
    shape = lines.shape
    parts = lines.reshape(PEERS, 1, -1)
    return lax.all_to_all(parts, CHIPS, 0, 0, tiled=True).reshape(shape)


def other_core(x):
    return lax.ppermute(x, CORE, [(0, 1), (1, 0)])


def body(panel, treat_start, loading_init, factor_init, unit_init, day_init):
    f_own, f_oth = gather_factors(factor_init)
    ts = treat_start.reshape(1, ROWS)
    panel, b, loading, a, tsb, *spreads = prep(
        panel, day_init.reshape(1, DAYS), loading_init, unit_init.reshape(1, ROWS), ts
    )
    for sweep in range(SWEEPS):
        sent, dhi_oth, dlo_oth, acc = first_other(panel, f_oth, b, a, tsb, *spreads)
        arrived = other_core(sent)
        kept, dhi_own, dlo_own, rm = first_own(panel, f_own, b, a, tsb, *spreads, loading, acc)
        summed = sum_and_copy(swap_chips(kept + arrived))
        own = swap_chips(summed)
        oth = other_core(own)
        ginv = gram_inverse(own)
        final = sweep == SWEEPS - 1
        b, loading, a, *rest = second(
            final, own, oth, ginv, f_own, f_oth, b, dhi_own, dlo_own, dhi_oth, dlo_oth, loading, a, rm
        )
        if not final:
            f_own, f_oth, *spreads = rest
    return (loading, rest[0].T, a.reshape(ROWS), b.reshape(DAYS))


def solution(mesh):
    finer = Mesh(
        mesh.devices.reshape(mesh.shape["gx"], mesh.shape["gy"], 4, 2), ("gx", "gy", "gz_0", "gz_1")
    )
    return jax.shard_map(
        body,
        mesh=finer,
        in_specs=(
            P(GX_GY_GZ, None),
            P(GX_GY_GZ),
            P(None, GX_GY_GZ),
            P(None, GX_GY_GZ),
            P(GX_GY_GZ),
            P(),
        ),
        out_specs=(P(None, GX_GY_GZ), P(None, GX_GY_GZ), P(GX_GY_GZ), P()),
        check_vma=False,
    )
```

```python
import functools

import jax
import jax.numpy as jnp
from jax import lax
from jax.experimental import pallas as pl
from jax.experimental.pallas import tpu as pltpu
from jax.sharding import Mesh
from jax.sharding import PartitionSpec as P

SWEEPS = 2
RIDGE = 1.0
GX_GY_GZ = ("gx", "gy", "gz_0", "gz_1")
CHIPS = ("gx", "gy", "gz_0")
CORE = "gz_1"

RANK = 64
ROWS = 256
DAYS = 4096
HALF = 2048
UNITS = 32768
BLK = 512
NBLK = HALF // BLK
PEERS = 64
CHUNK = 17
BROWS = 16 * CHUNK
PAY = PEERS * CHUNK
F32 = jnp.float32
BF = jnp.bfloat16


def dot(x, y, dims=((1,), (0,))):
    return lax.dot_general(x, y, (dims, ((), ())), preferred_element_type=F32)


def dot_exact(x, y, dims=((1,), (0,))):
    return lax.dot_general(x, y, (dims, ((), ())), preferred_element_type=F32, precision=lax.Precision.HIGHEST)


def split(x):
    hi = x.astype(BF)
    return hi, (x - hi.astype(F32)).astype(BF)


def split_rows(x):
    hi = x.astype(BF).astype(F32)
    mid = (x - hi).astype(BF).astype(F32)
    return [hi, mid, x - hi - mid]


def pair_inverse(a, b, d):
    q = 1.0 / (a * d - b * b)
    return d * q, -b * q, a * q


def block_inverse(p):
    a0, a1, a2 = pair_inverse(p[0, 0], p[0, 1], p[1, 1])
    top, low = (a0, a1), (a1, a2)
    ab = [[r[0] * p[0, c] + r[1] * p[1, c] for c in (2, 3)] for r in (top, low)]
    s00 = p[2, 2] - (p[0, 2] * ab[0][0] + p[1, 2] * ab[1][0])
    s01 = p[2, 3] - (p[0, 2] * ab[0][1] + p[1, 2] * ab[1][1])
    s11 = p[3, 3] - (p[0, 3] * ab[0][1] + p[1, 3] * ab[1][1])
    s0, s1, s2 = pair_inverse(s00, s01, s11)
    k = [[-(r[0] * s0 + r[1] * s1), -(r[0] * s1 + r[1] * s2)] for r in ab]
    c00 = a0 - (k[0][0] * ab[0][0] + k[0][1] * ab[0][1])
    c01 = a1 - (k[0][0] * ab[1][0] + k[0][1] * ab[1][1])
    c11 = a2 - (k[1][0] * ab[1][0] + k[1][1] * ab[1][1])
    return [
        [c00, c01, k[0][0], k[0][1]],
        [c01, c11, k[1][0], k[1][1]],
        [k[0][0], k[1][0], s0, s1],
        [k[0][1], k[1][1], s1, s2],
    ]


def inverse(m):
    n = m.shape[0]
    row = lax.broadcasted_iota(jnp.int32, (n, n), 0)
    col = lax.broadcasted_iota(jnp.int32, (n, n), 1)
    w = jnp.concatenate([m, (row == col).astype(F32)], axis=1)
    w = [w[8 * t : 8 * t + 8] for t in range(n // 8)]
    rows = lax.broadcasted_iota(jnp.int32, (8, 2 * n), 0)
    full = lambda v: jnp.broadcast_to(v, (8, 2 * n))
    for k in range(0, n, 4):
        at, r0 = k // 8, k % 8
        c = [[full(v[:, k + j : k + j + 1]) for j in range(4)] for v in w]
        lines = [w[at][r0 + i : r0 + i + 1] for i in range(4)]
        p = block_inverse({(i, j): c[at][j][r0 + i : r0 + i + 1] for i in range(4) for j in range(i, 4)})
        t = [(p[i][0] * lines[0] + p[i][1] * lines[1]) + (p[i][2] * lines[2] + p[i][3] * lines[3]) for i in range(4)]
        for g in range(n // 8):
            w[g] = w[g] - ((c[g][0] * t[0] + c[g][1] * t[1]) + (c[g][2] * t[2] + c[g][3] * t[3]))
        for i in range(4):
            w[at] = jnp.where(rows == r0 + i, t[i], w[at])
    return jnp.concatenate(w, axis=0)[:, n:]


def spread(lv, av, lt, lw, gp):
    lhi, llo = split(lv)
    hi32, lo32 = lhi.astype(F32), llo.astype(F32)
    ones = jnp.ones((3, ROWS), F32)
    k_rows = [hi32, hi32, lo32] + split_rows(av) + [ones, jnp.zeros((58, ROWS), F32)]
    lt[...] = jnp.concatenate(k_rows, axis=0).T.astype(BF)
    lw[0:64] = lhi
    lw[64:128] = llo
    lw[128:144] = jnp.ones((16, ROWS), BF)
    last = ((1,), (1,))
    both = jnp.concatenate([lhi, llo], axis=0)
    g = dot(both, lhi, last)
    g = g[0:64] + g[64:128] + dot(lhi, llo, last)
    gp[0:32] = jnp.concatenate([g[0:32], g[32:64]], axis=1)
    l1 = dot(jnp.ones((16, ROWS), BF), both, last)[0:1]
    gp[32:33] = jnp.concatenate([l1[:, 0:64] + l1[:, 64:128], jnp.zeros((1, 64), F32)], axis=1)


SPREAD = [((ROWS, 256), BF), ((144, ROWS), BF), ((40, 128), F32)]


def prep_kernel(panel, b, l, a, ts, panel_out, b_out, l_out, a_out, tsb, lt, lw, gp, ts_in, sems):
    pairs = ((panel, panel_out), (b, b_out), (l, l_out), (a, a_out), (ts, ts_in))
    moves = [pltpu.make_async_copy(src, dst, sems.at[i]) for i, (src, dst) in enumerate(pairs)]
    for move in moves:
        move.start()
    for move in moves[1:]:
        move.wait()
    tsb[...] = jnp.broadcast_to(ts_in[...].astype(F32), (128, ROWS)).T
    spread(l_out[...], a_out[...], lt, lw, gp)
    moves[0].wait()


def prep(*operands):
    outs = [((ROWS, DAYS), F32), ((1, DAYS), F32), ((RANK, ROWS), F32), ((1, ROWS), F32), ((ROWS, 128), F32)] + SPREAD
    return pl.pallas_call(
        prep_kernel,
        in_specs=[pl.BlockSpec(memory_space=pltpu.HBM)] * 5,
        out_specs=[vmem()] * len(outs),
        out_shape=[pltpu.VMEM(shape, dtype) for shape, dtype in outs],
        scratch_shapes=[pltpu.VMEM((1, ROWS), jnp.int32), pltpu.SemaphoreType.DMA((5,))],
        compiler_params=pltpu.CompilerParams(vmem_limit_bytes=16 << 20),
        name="prep",
    )(*[pltpu.with_memory_space_constraint(x, pltpu.HBM) for x in operands])


def first_kernel(panel, f, b, a, tsb, lt, lw, gp, *rest, own):
    if own:
        l, acc_in, out, dhi, dlo, rm = rest
    else:
        out, dhi, dlo, acc_out = rest
    k = lax.axis_index(CORE)
    half = k if own else 1 - k
    start = pl.multiple_of(half * HALF, HALF)
    lane = lax.broadcasted_iota(jnp.int32, (ROWS, 128), 1)
    left = tsb[...] - (lane + start).astype(F32)
    run = acc_in[...] if own else jnp.zeros((ROWS, 128), F32)
    a_sum = jnp.broadcast_to(jnp.sum(a[...], axis=1, keepdims=True), (1, 128))

    def fit(j):
        fhi, flo = split(f[:, BLK * j : BLK * (j + 1)])
        bv = b[:, pl.ds(start + BLK * j, BLK)]
        aux = jnp.concatenate([jnp.ones((3, BLK), F32)] + split_rows(bv) + [jnp.zeros((58, BLK), F32)], axis=0)
        return dot(lt[...], jnp.concatenate([fhi, flo, fhi, aux.astype(BF)], axis=0))

    def weigh(j):
        whole = slice(BLK * j, BLK * (j + 1))
        r1 = dot(lw[...], dhi[:, whole])
        r2 = dot(lw[...], dlo[:, whole])
        w = r1[0:64] + r1[64:128] + r2[0:64]
        day_sum = r1[128:129] + r2[128:129]
        extra = [day_sum[:, 128 * q : 128 * (q + 1)] for q in range(4)]
        line = gp[32:33, :]
        if own and j == NBLK - 1:
            means = dot_exact(jnp.ones((8, 128), F32), run, ((1,), (1,))) * (1.0 / DAYS)
            rm[...] = means[0:1]
            lr = dot_exact(means, l[...], ((1,), (1,)))[0:1]
            line = jnp.concatenate([line[:, 0:64], lr], axis=1)
        extra += [gp[8 * j : 8 * j + 8], line, a_sum, jnp.zeros((2, 128), F32)]
        extra = jnp.concatenate(extra, axis=0)
        for i in range(8):
            for t in range(2):
                at = BROWS * j + CHUNK * (2 * i + t)
                out[at : at + 8, :] = w[8 * i : 8 * i + 8, 256 * t : 256 * t + 128]
                out[at + 8 : at + 16, :] = w[8 * i : 8 * i + 8, 256 * t + 128 : 256 * t + 256]
                out[at + 16 : at + 17, :] = extra[2 * i + t : 2 * i + t + 1]

    s = fit(0)
    for j in range(NBLK):
        following = fit(j + 1) if j + 1 < NBLK else None
        for q in range(BLK // 128):
            at = BLK * j + 128 * q
            cols = slice(at, at + 128)
            x = panel[:, pl.ds(start + at, 128)]
            d = jnp.where(left > float(at), x - s[:, 128 * q : 128 * (q + 1)], 0.0)
            hi, lo = split(d)
            dhi[:, cols] = hi
            dlo[:, cols] = lo
            run = run + d
        s = following
        if j:
            weigh(j - 1)
    weigh(NBLK - 1)
    if not own:
        acc_out[...] = run


def vmem():
    return pl.BlockSpec(memory_space=pltpu.VMEM)


def device_index():
    gx, gy, gz_0, gz_1 = [lax.axis_index(axis) for axis in GX_GY_GZ]
    return ((gx * 4 + gy) * 4 + gz_0) * 2 + gz_1


def call(kernel, name, operands, outs, scratch=(), place=pltpu.VMEM):
    return pl.pallas_call(
        kernel,
        in_specs=[vmem()] * len(operands),
        out_specs=[vmem()] * len(outs),
        out_shape=[place(shape, dtype) for shape, dtype in outs],
        scratch_shapes=list(scratch),
        compiler_params=pltpu.CompilerParams(vmem_limit_bytes=16 << 20),
        name=name,
    )(*[pltpu.with_memory_space_constraint(x, pltpu.VMEM) for x in operands])


def first_other(panel, f, b, a, *spreads):
    outs = [((PAY, 128), F32), ((ROWS, HALF), BF), ((ROWS, HALF), BF), ((ROWS, 128), F32)]
    return call(functools.partial(first_kernel, own=False), "first_other", [panel, f, b, a, *spreads], outs)


def first_own(panel, f, b, a, *rest):
    outs = [((PAY, 128), F32), ((ROWS, HALF), BF), ((ROWS, HALF), BF), ((1, ROWS), F32)]
    return call(functools.partial(first_kernel, own=True), "first_own", [panel, f, b, a, *rest], outs)


def sum_kernel(x, out):
    slab = x[0 : 8 * CHUNK, :]
    for g in range(1, 8):
        slab = slab + x[8 * CHUNK * g : 8 * CHUNK * (g + 1), :]
    total = slab[0:CHUNK]
    for c in range(1, 8):
        total = total + slab[CHUNK * c : CHUNK * (c + 1)]
    slab = jnp.concatenate([total] * 8, axis=0)
    for g in range(8):
        out[8 * CHUNK * g : 8 * CHUNK * (g + 1), :] = slab


def sum_and_copy(x):
    return call(sum_kernel, "sum_and_copy", [x], [((PAY, 128), F32)])[0]


def extra_row(x, j, e):
    at = BROWS * j + CHUNK * e + 16
    return x[at : at + 1, :]


def gram_kernel(x, out):
    packed = jnp.concatenate([extra_row(x, j, 4 + e) for j in range(4) for e in range(8)], axis=0)
    g = jnp.concatenate([packed[:, 0:64], packed[:, 64:128]], axis=0)
    row = lax.broadcasted_iota(jnp.int32, (RANK, RANK), 0)
    col = lax.broadcasted_iota(jnp.int32, (RANK, RANK), 1)
    out[...] = inverse(g + jnp.where(row == col, RIDGE, 0.0))


def gram_inverse(x):
    return call(gram_kernel, "gram_inverse", [x], [((RANK, RANK), F32)])[0]


def second_kernel(own, oth, ginv, f_own, f_oth, b_ref, dhi_own, dlo_own, dhi_oth, dlo_oth, l, a, rm, *rest, final):
    if final:
        bn, ln, an, shard, fn_own, fn_oth, bt, new_rows, turn = rest
    else:
        bn, ln, an, fn_own, fn_oth, lt, lw, gp, bt, new_rows = rest
    k = lax.axis_index(CORE)
    starts = [pl.multiple_of(k * HALF, HALF), pl.multiple_of((1 - k) * HALF, HALF)]
    sums = [jnp.concatenate([extra_row(x, j, q) for j in range(4) for q in range(4)], axis=1) for x in (own, oth)]
    mean_d = jnp.sum(sums[0] + sums[1], axis=1, keepdims=True) * (1.0 / (UNITS * DAYS))
    mean_b = jnp.sum(b_ref[...], axis=1, keepdims=True) * (1.0 / DAYS)
    mean_a = extra_row(own, 3, 13)[:, 0:1] * (1.0 / UNITS)
    lane = lax.broadcasted_iota(jnp.int32, (1, 128), 1)
    l_own, l_oth = extra_row(own, 3, 12), extra_row(oth, 3, 12)
    lines = l_own + jnp.where(lane >= 64, l_oth, 0.0)
    turned = jnp.broadcast_to(lines, (128, 128)).T
    l1 = turned[0:64, 0:1]
    u = (mean_d + mean_a) * l1 - turned[64:128, 0:1]
    ghi, glo = split(ginv[...])
    gcat = jnp.concatenate([ghi, ghi, glo], axis=1)
    f1 = jnp.zeros((RANK, 128), F32)
    fb = jnp.zeros((RANK, 128), F32)
    for side, (x, f, fn, col, start) in enumerate(
        ((own, f_own, fn_own, sums[0], starts[0]), (oth, f_oth, fn_oth, sums[1], starts[1]))
    ):
        v = mean_d + mean_b - col * (1.0 / UNITS)
        bn[:, pl.ds(start, HALF)] = b_ref[:, pl.ds(start, HALF)] - v
        def solved(j, x=x, f=f, v=v):
            cols = slice(BLK * j, BLK * (j + 1))
            lines = []
            for i in range(8):
                tiles = []
                for t in range(2):
                    at = BROWS * j + CHUNK * (2 * i + t)
                    tiles += [x[at : at + 8, :], x[at + 8 : at + 16, :]]
                lines.append(jnp.concatenate(tiles, axis=1))
            fv = f[:, cols]
            r = jnp.concatenate(lines, axis=0) + u + l1 * v[:, cols] - fv
            rhi, rlo = split(r)
            return fv, dot(gcat, jnp.concatenate([rhi, rlo, rhi], axis=0))

        pending = solved(0)
        for j in range(NBLK):
            cols = slice(BLK * j, BLK * (j + 1))
            fv, step = pending
            if j + 1 < NBLK:
                pending = solved(j + 1)
            new = fv + step
            fn[:, cols] = new
            nhi, nlo = split(new)
            ohi, olo = split(fv)
            both = jnp.concatenate([nhi, nlo, ohi, olo], axis=0).T
            at = HALF * side + BLK * j
            bt[at : at + BLK, :] = both
            new_rows[:, at : at + BLK] = jnp.concatenate([nhi, nlo], axis=0)
            nb = new * v[:, cols]
            for q in range(BLK // 128):
                f1 = f1 + new[:, 128 * q : 128 * (q + 1)]
                fb = fb + nb[:, 128 * q : 128 * (q + 1)]
    hx = dot(new_rows[...], bt[...])
    f1 = jnp.sum(f1, axis=1, keepdims=True)
    fb = jnp.sum(fb, axis=1, keepdims=True)
    da = mean_d + mean_a - rm[...]
    a_new = a[...] - da
    an[...] = a_new
    row = lax.broadcasted_iota(jnp.int32, (RANK, RANK), 0)
    col = lax.broadcasted_iota(jnp.int32, (RANK, RANK), 1)
    h = hx[0:64, 0:64] + hx[0:64, 64:128] + hx[64:128, 0:64]
    xn = hx[0:64, 128:192] + hx[0:64, 192:256] + hx[64:128, 128:192]
    z = jnp.zeros((RANK, ROWS), F32)
    for at, hi, lo in ((0, dhi_own, dlo_own), (HALF, dhi_oth, dlo_oth)):
        days = slice(at, at + HALF)
        part = dot(new_rows[:, days], hi[...], ((1,), (1,)))
        z = z + part[0:64] + part[64:128] + dot(new_rows[0:64, days], lo[...], ((1,), (1,)))
    hinv = inverse(h + jnp.where(row == col, RIDGE, 0.0))
    p = dot_exact(xn, l[...]) + f1 * da + fb + z
    l_new = dot_exact(hinv, p)
    ln[...] = l_new
    if final:
        device = device_index()
        tile = pl.multiple_of(128 * ((device & 63) // 4), 128)
        mine = jnp.where(device // 64 == k, fn_own[:, pl.ds(tile, 128)], fn_oth[:, pl.ds(tile, 128)])
        turn[...] = mine.T
        shard[...] = turn[pl.ds(pl.multiple_of(32 * (device & 3), 32), 32), :]
    else:
        spread(l_new, a_new, lt, lw, gp)


def second(final, *operands):
    outs = [((1, DAYS), F32), ((RANK, ROWS), F32), ((1, ROWS), F32)]
    kernel = functools.partial(second_kernel, final=final)
    half = ((RANK, HALF), F32)
    work = [pltpu.VMEM((DAYS, 256), BF), pltpu.VMEM((128, DAYS), BF)]
    if final:
        scratch = [pltpu.VMEM(*half), pltpu.VMEM(*half), *work, pltpu.VMEM((128, RANK), F32)]
        outs = outs + [((32, RANK), F32)]
        return call(kernel, "second_last", operands, outs, scratch, jax.ShapeDtypeStruct)
    return call(kernel, "second", operands, outs + [half, half] + SPREAD, work)


def pack_kernel(x, out):
    v = x[...].T
    packed = jnp.concatenate([v[16 * q : 16 * q + 16] for q in range(4)], axis=1)
    packed = pltpu.roll(packed, 32 * (device_index() & 3), 1)
    for c in range(PEERS):
        out[16 * c : 16 * c + 16, :] = packed


def unpack_kernel(own, oth, f_own, f_oth):
    k = lax.axis_index(CORE)
    even = k == 0
    slot = lax.broadcasted_iota(jnp.int32, (16, 128), 1) // 32
    for j in range(16):
        for dst, half in ((f_own, k), (f_oth, 1 - k)):
            parts = []
            for m in range(4):
                at = pl.multiple_of((half * 32 + 2 * j + m // 2) * 16, 16)
                x, y = own[pl.ds(at, 16), :], oth[pl.ds(at, 16), :]
                parts.append(jnp.where(even, x, y) if m % 2 == 0 else jnp.where(even, y, x))
            for q in range(4):
                total = parts[-q % 4]
                for t in range(1, 4):
                    total = jnp.where(slot == t, parts[(t - q) % 4], total)
                if q:
                    total = pltpu.roll(total, 128 - 32 * q, 1)
                dst[16 * q : 16 * q + 16, 128 * j : 128 * j + 128] = total


def gather_factors(f):
    lines = call(pack_kernel, "pack_factors", [f.T], [((PEERS * 16, 128), F32)])[0]
    own = swap_chips(lines)
    oth = other_core(own)
    return call(unpack_kernel, "unpack_factors", [own, oth], [((RANK, HALF), F32)] * 2)


def swap_chips(lines):
    shape = lines.shape
    parts = lines.reshape(PEERS, 1, -1)
    return lax.all_to_all(parts, CHIPS, 0, 0, tiled=True).reshape(shape)


def other_core(x):
    return lax.ppermute(x, CORE, [(0, 1), (1, 0)])


def body(panel, treat_start, loading_init, factor_init, unit_init, day_init):
    f_own, f_oth = gather_factors(factor_init)
    ts = treat_start.reshape(1, ROWS)
    panel, b, loading, a, tsb, *spreads = prep(
        panel, day_init.reshape(1, DAYS), loading_init, unit_init.reshape(1, ROWS), ts
    )
    for sweep in range(SWEEPS):
        sent, dhi_oth, dlo_oth, acc = first_other(panel, f_oth, b, a, tsb, *spreads)
        arrived = other_core(sent)
        kept, dhi_own, dlo_own, rm = first_own(panel, f_own, b, a, tsb, *spreads, loading, acc)
        summed = sum_and_copy(swap_chips(kept + arrived))
        own = swap_chips(summed)
        oth = other_core(own)
        ginv = gram_inverse(own)
        final = sweep == SWEEPS - 1
        b, loading, a, *rest = second(
            final, own, oth, ginv, f_own, f_oth, b, dhi_own, dlo_own, dhi_oth, dlo_oth, loading, a, rm
        )
        if not final:
            f_own, f_oth, *spreads = rest
    return (loading, rest[0].T, a.reshape(ROWS), b.reshape(DAYS))


def solution(mesh):
    finer = Mesh(
        mesh.devices.reshape(mesh.shape["gx"], mesh.shape["gy"], 4, 2), ("gx", "gy", "gz_0", "gz_1")
    )
    return jax.shard_map(
        body,
        mesh=finer,
        in_specs=(
            P(GX_GY_GZ, None),
            P(GX_GY_GZ),
            P(None, GX_GY_GZ),
            P(None, GX_GY_GZ),
            P(GX_GY_GZ),
            P(),
        ),
        out_specs=(P(None, GX_GY_GZ), P(None, GX_GY_GZ), P(GX_GY_GZ), P()),
        check_vma=False,
    )
```
